256 devices in a mesh: rows: 64 (over x, z, core), cols: 4 (over y).
Axes of the slice: x: 4, y: 4, z: 8, core: 2. Of those that a mesh axis runs over, the one named last changes fastest.
Arguments:
- hidden_acts: bfloat16 [1, 27648, 2560], P(None, 'rows'), may hold values from -17 to 17
- out_grads: bfloat16 [1, 2560, 5120], P(None, None, 'cols'), may hold values from -13 to 13
- row_signs: int32 [27648], P('rows'), may hold values from -1 to 1, as said below
- kept_index: int32 [16384], P('rows'), may hold values from 0 to 32767, as said below
Outputs:
- sketch: float32 [1, 16384, 5120], P(None, 'rows', 'cols')
The draws below stay inside these ranges and needn't reach their ends.
Inputs may be any that keep to these rules, and one draw needn't show every extreme that they name: `row_signs`: each entry is +1 or -1. `kept_index`: for each b and each s = 0 .. 63, entries b * 256 + s * 4 to b * 256 + (s + 1) * 4 - 1 are distinct padded rows within b * 512 + s * 8 to b * 512 + (s + 1) * 8 - 1.
All inputs are finite; a program needn't handle non-finite values.
Results may differ from the reference program's by a relative error of at most 0.0003.
Values sent between devices are 32-bit elements; how exact they have to be, the bound alone decides.
No kernel may reach another device: no remote copies, remote signals or barrier semaphores. Data moves between devices by JAX's collectives and lax.ppermute only.
A program may use at most 64 MiB of HBM per device.

```python
import jax
import jax.numpy as jnp
from jax import lax

D = 5120
FF = 27648
PADDED = 32768
KEPT = 16384
TOKENS = 2560
EXAMPLES = 1
PAD_DEV = 512
KEEP_DEV = 256
N_ROWS = 64
N_COLS = 4


def draw_hidden_acts(key, part):
    first, second = jax.random.split(jax.random.fold_in(key, 11), 2)
    position = jnp.arange(FF, dtype=jnp.float32) / FF
    level = 0.5 * position + 0.5 * jax.random.uniform(first, (FF,), jnp.float32)
    row_scale = 10.0 ** level
    base = jnp.clip(jax.random.normal(second, (EXAMPLES, FF, TOKENS), jnp.float32), -5.0, 5.0)
    return (base * row_scale[None, :, None] / 3.0).astype(jnp.bfloat16)


def draw_out_grads(key, part):
    first, second = jax.random.split(jax.random.fold_in(key, 23), 2)
    col_scale = 10.0 ** jax.random.uniform(first, (D,), jnp.float32)
    base = jnp.clip(jax.random.normal(second, (EXAMPLES, TOKENS, D), jnp.float32), -5.0, 5.0)
    return (base * col_scale[None, None, :] / 4.0).astype(jnp.bfloat16)


def draw_row_signs(key, part):
    coins = jax.random.randint(jax.random.fold_in(key, 37), (FF,), 0, 2, dtype=jnp.int32)
    return (2 * coins - 1).astype(jnp.int32)


def draw_kept_index(key, part):
    blocks = PADDED // PAD_DEV
    segment = PAD_DEV // N_ROWS
    share = KEEP_DEV // N_ROWS
    keys = jax.random.split(jax.random.fold_in(key, 41), blocks * N_ROWS)

    def choose(segment_key):
        return jax.random.permutation(segment_key, segment)[:share].astype(jnp.int32)
    chosen = jax.vmap(choose)(keys).reshape(blocks, N_ROWS, share)
    block_offsets = jnp.arange(blocks, dtype=jnp.int32)[:, None, None] * PAD_DEV
    segment_offsets = jnp.arange(N_ROWS, dtype=jnp.int32)[None, :, None] * segment
    return (chosen + block_offsets + segment_offsets).reshape(KEPT).astype(jnp.int32)


def setup_inputs(seed: int = 0) -> dict:
    seeds = jax.random.split(jax.random.key(seed), 5)
    return {
        "hidden_acts": draw_hidden_acts(jax.random.fold_in(seeds[4], 71), 0),
        "out_grads": draw_out_grads(jax.random.fold_in(seeds[4], 71), 0),
        "row_signs": draw_row_signs(jax.random.fold_in(seeds[4], 71), 0),
        "kept_index": draw_kept_index(jax.random.fold_in(seeds[4], 71), 0),
    }


epsilon = 1e-06

def sylvester(length):
    indices = jnp.arange(length, dtype=jnp.int32)
    intersection = indices[:, None] & indices[None, :]
    parity = jnp.zeros_like(intersection)
    for bit_level in range(length.bit_length() - 1):
        parity = parity ^ intersection >> bit_level & 1
    return (1 - 2 * parity).astype(jnp.float32)

def reference(hidden_acts, out_grads, row_signs, kept_index):
    pad_rows = PADDED // N_ROWS
    own_rows = FF // N_ROWS
    width = D // N_COLS
    inner_table = sylvester(pad_rows)
    outer_table = sylvester(N_ROWS)
    sign_column = row_signs[:, None].astype(jnp.float32)
    results = []
    for example in range(EXAMPLES):
        squares_all = jnp.zeros((), jnp.float32)
        columns = []
        for block_index in range(N_COLS):
            grads_block = out_grads[example][:, block_index * width:(block_index + 1) * width]
            gradient = jnp.dot(hidden_acts[example], grads_block, preferred_element_type=jnp.float32)
            squares_all = squares_all + jnp.sum(gradient * gradient)
            signed = gradient * sign_column
            stacked = signed.reshape(N_ROWS, own_rows, width)
            stacked = jnp.pad(stacked, ((0, 0), (0, pad_rows - own_rows), (0, 0)))
            inner_mixed = jnp.einsum('ij,bjc->bic', inner_table, stacked, precision=lax.Precision.HIGHEST)
            mixed_rows = jnp.einsum('ab,bic->aic', outer_table, inner_mixed, precision=lax.Precision.HIGHEST)
            mixed_rows = mixed_rows.reshape(PADDED, width)
            columns.append(jnp.take(mixed_rows, kept_index, axis=0))
        inv_norm = 1.0 / jnp.sqrt(squares_all / D + epsilon)
        results.append(jnp.concatenate(columns, axis=1) * inv_norm)
    return jnp.stack(results)
```

```python
import functools

import jax
import jax.numpy as jnp
import numpy as np
from jax import lax
from jax.experimental import pallas as pl
from jax.experimental.pallas import tpu as pltpu
from jax.sharding import PartitionSpec as P

D = 5120
PADDED = 32768

epsilon = 1e-06


def sylvester(length):
    i = np.arange(length)
    common = i[:, None] & i[None, :]
    parity = np.zeros_like(common)
    for bit in range(length.bit_length() - 1):
        parity ^= common >> bit & 1
    return 1 - 2 * parity


def mix_kernel(segments_ref, position_ref, kept_ref, work_ref):
    blocks = segments_ref.shape[0]
    share = kept_ref.shape[1]
    half = blocks // 8
    for high in range(8):
        rows = [segments_ref[high * half + low] for low in range(half)]
        for bit in (1, 2, 4):
            rows = [
                rows[i ^ bit] - rows[i] if i & bit else rows[i] + rows[i ^ bit]
                for i in range(half)
            ]
        for low in range(half):
            work_ref[high * half + low] = rows[low]
    for low in range(half):
        rows = [work_ref[high * half + low] for high in range(8)]
        for bit in (1, 2, 4):
            rows = [
                rows[i ^ bit] - rows[i] if i & bit else rows[i] + rows[i ^ bit]
                for i in range(8)
            ]
        for high in range(8):
            block = high * half + low
            picked = jnp.take_along_axis(
                rows[high], position_ref[block], axis=0, mode="promise_in_bounds"
            )
            kept_ref[block] = picked[:share]


def mix(segments, position, share):
    blocks, segment, width = segments.shape
    return pl.pallas_call(
        mix_kernel,
        grid=(width // 128,),
        in_specs=[
            pl.BlockSpec((blocks, segment, 128), lambda i: (0, 0, i)),
            pl.BlockSpec((blocks, segment, 128), lambda i: (0, 0, 0)),
        ],
        out_specs=pl.BlockSpec((blocks, share, 128), lambda i: (0, 0, i)),
        out_shape=jax.ShapeDtypeStruct((blocks, share, width), jnp.float32),
        scratch_shapes=[pltpu.VMEM((blocks, segment, 128), jnp.float32)],
    )(segments, position)


def sketch_kernel(col_ref, scale_ref, *refs):
    parts = refs[:-3]
    grads_ref, out_ref, terms_ref = refs[-3:]
    count = len(parts)
    rows, width = parts[0].shape

    @pl.when(pl.program_id(0) == 0)
    def _():
        for shift in range(count):
            source = lax.rem(col_ref[0] + count - shift, count)
            at = pl.ds(pl.multiple_of(source * width, 128), width)
            value = parts[shift][...]
            coarse = value.astype(jnp.bfloat16)
            terms_ref[:rows, at] = coarse
            terms_ref[rows:, at] = (value - coarse.astype(jnp.float32)).astype(jnp.bfloat16)

    both = jnp.dot(terms_ref[...], grads_ref[...], preferred_element_type=jnp.float32)
    out_ref[...] = (both[:rows] + both[rows:]) * scale_ref[0]


def sketch(col, scale, parts, grads):
    rows, width = parts[0].shape
    tokens, columns = grads.shape
    tile = 256
    return pl.pallas_call(
        sketch_kernel,
        grid=(columns // tile,),
        in_specs=[
            pl.BlockSpec(memory_space=pltpu.SMEM),
            pl.BlockSpec(memory_space=pltpu.SMEM),
            *[pl.BlockSpec((rows, width), lambda i: (0, 0))] * len(parts),
            pl.BlockSpec((tokens, tile), lambda i: (0, i)),
        ],
        out_specs=pl.BlockSpec((rows, tile), lambda i: (0, i)),
        out_shape=jax.ShapeDtypeStruct((rows, columns), jnp.float32),
        scratch_shapes=[pltpu.VMEM((2 * rows, tokens), jnp.bfloat16)],
    )(col, scale, *parts, grads)


def col_shift(value, shift):
    cols = lax.axis_size("cols")
    return lax.ppermute(value, "cols", [(c, (c + shift) % cols) for c in range(cols)])


def local(hidden_acts, out_grads, row_signs, kept_index):
    row_devices = lax.axis_size("rows")
    cols = lax.axis_size("cols")
    block = lax.axis_index("rows")
    col = lax.axis_index("cols")
    pad_rows = PADDED // row_devices
    own_rows, tokens = hidden_acts.shape[1:]
    segment = pad_rows // row_devices
    share = kept_index.shape[0] // row_devices
    width = tokens // cols
    acts, grads = hidden_acts[0], out_grads[0]

    table = jnp.asarray(sylvester(pad_rows)[:, :own_rows], dtype=jnp.bfloat16)
    table = table * row_signs.astype(jnp.bfloat16)[None, :]
    own = lax.dynamic_slice(acts, (0, col * width), (own_rows, width))
    inner = jnp.dot(table, own, preferred_element_type=jnp.float32)
    segments = lax.all_to_all(
        inner.reshape(row_devices, segment, width), "rows", 0, 0, tiled=True
    )

    gradient = jnp.dot(acts, grads, preferred_element_type=jnp.float32)
    squares = jnp.sum(gradient * gradient)
    first = block * pad_rows + segment * jnp.arange(row_devices, dtype=jnp.int32)
    position = kept_index.reshape(row_devices, share) - first[:, None]
    notes = jnp.concatenate(
        [
            position.astype(jnp.float32),
            jnp.broadcast_to(squares, (row_devices, 128 - share)),
        ],
        axis=1,
    )
    notes = lax.all_to_all(notes[:, None, :], "rows", 0, 0, tiled=True)
    squares = jnp.broadcast_to(jnp.sum(notes[:, 0, share]), (8, 128))
    squares = squares + lax.ppermute(squares, "cols", [(c, c ^ 1) for c in range(cols)])
    squares = squares + lax.ppermute(squares, "cols", [(c, c ^ 2) for c in range(cols)])
    scale = lax.rsqrt(squares[0, :1] / D + epsilon)
    position = notes[:, 0, :share].astype(jnp.int32)
    position = jnp.pad(position, ((0, 0), (0, segment - share)))
    position = jnp.broadcast_to(position[:, :, None], (row_devices, segment, 128))

    kept = mix(segments, position, share)
    kept = lax.all_to_all(kept, "rows", 0, 0, tiled=True)
    kept = kept.reshape(row_devices * share, width)
    parts = [kept] + [col_shift(kept, shift) for shift in range(1, cols)]
    return sketch(col[None], scale, parts, grads)[None]


def solution(mesh):
    return jax.shard_map(
        local,
        mesh=mesh,
        in_specs=(P(None, "rows", None), P(None, None, "cols"), P("rows"), P("rows")),
        out_specs=P(None, "rows", "cols"),
        check_vma=False,
    )
```

```python
import functools

import jax
import jax.numpy as jnp
import numpy as np
from jax import lax
from jax.experimental import pallas as pl
from jax.experimental.pallas import tpu as pltpu
from jax.sharding import PartitionSpec as P


D = 5120
PADDED = 32768

epsilon = 1e-06


def sylvester(length):
    i = np.arange(length)
    common = i[:, None] & i[None, :]
    parity = np.zeros_like(common)
    for bit in range(length.bit_length() - 1):
        parity ^= common >> bit & 1
    return 1 - 2 * parity


LANES = 128
SUBLANES = 8
CHUNKS = (640,)

WHOLE = pl.BlockSpec(memory_space=pltpu.VMEM)
SCALAR = pl.BlockSpec(memory_space=pltpu.SMEM)


def butterfly(rows):
    count = len(rows)
    bit = 1
    while bit < count:
        rows = [
            rows[i ^ bit] - rows[i] if i & bit else rows[i] + rows[i ^ bit]
            for i in range(count)
        ]
        bit *= 2
    return rows


def inner_kernel(blocks, col_ref, table_ref, signs_ref, kept_ref, acts_ref, out_ref):
    tiles = acts_ref.shape[2] // LANES
    stride = tiles * SUBLANES + 1
    table = table_ref[...] * signs_ref[...].astype(jnp.float32).astype(jnp.bfloat16)
    mixed = jnp.dot(table, acts_ref[0], preferred_element_type=jnp.float32)
    kept = kept_ref[...].astype(jnp.float32)
    share = kept.size // blocks
    for block in range(blocks):
        rows = slice(block * SUBLANES, (block + 1) * SUBLANES)
        for tile in range(tiles):
            out_ref[pl.ds(block * stride + tile * SUBLANES, SUBLANES), :] = mixed[
                rows, tile * LANES:(tile + 1) * LANES
            ]
        row = block * share // LANES
        out_ref[pl.ds((block + 1) * stride - 1, 1), :] = kept[row:row + 1]


def inner(col, table, signs, kept, acts, blocks, width):
    own_rows = acts.shape[1]
    rows = blocks * (width // LANES * SUBLANES + 1)
    return pl.pallas_call(
        functools.partial(inner_kernel, blocks),
        grid_spec=pltpu.PrefetchScalarGridSpec(
            num_scalar_prefetch=1,
            grid=(1,),
            in_specs=[
                pl.BlockSpec(table.shape, lambda i, c: (0, 0)),
                pl.BlockSpec(signs.shape, lambda i, c: (0, 0)),
                pl.BlockSpec(kept.shape, lambda i, c: (0, 0)),
                pl.BlockSpec((1, own_rows, width), lambda i, c: (0, 0, c[0])),
            ],
            out_specs=pl.BlockSpec((rows, LANES), lambda i, c: (0, 0)),
        ),
        out_shape=jax.ShapeDtypeStruct((rows, LANES), jnp.float32),
    )(col, table, signs, kept, acts)


def mix_kernel(first, tiles, block_ref, segments_ref, kept_ref, position_ref, work_ref):
    blocks, share, width = kept_ref.shape
    low_count = blocks // 8
    stride = tiles * SUBLANES + 1

    sublane = lax.broadcasted_iota(jnp.int32, (SUBLANES, LANES), 0)
    lane = lax.rem(block_ref[0], LANES // share) * share + jnp.minimum(sublane, share - 1)
    for block in range(blocks):
        row = segments_ref[pl.ds((block + 1) * stride - 1, 1), :]
        row = jnp.broadcast_to(row, (SUBLANES, LANES)).astype(jnp.int32) & (SUBLANES - 1)
        position_ref[block] = jnp.take_along_axis(
            row, lane, axis=1, mode="promise_in_bounds"
        )

    for tile in range(width // LANES):
        at = slice(tile * LANES, (tile + 1) * LANES)
        for high in range(8):
            rows = butterfly(
                [
                    segments_ref[
                        pl.ds(
                            (high * low_count + low) * stride + (first + tile) * SUBLANES,
                            SUBLANES,
                        ),
                        :,
                    ]
                    for low in range(low_count)
                ]
            )
            for low in range(low_count):
                work_ref[high * low_count + low] = rows[low]
        for low in range(low_count):
            rows = butterfly([work_ref[high * low_count + low] for high in range(8)])
            for high in range(8):
                block = high * low_count + low
                picked = jnp.take_along_axis(
                    rows[high], position_ref[block], axis=0, mode="promise_in_bounds"
                )
                kept_ref[block, :, at] = picked[:share]


def mix(block, segments, blocks, share, tiles, start, width):
    return pl.pallas_call(
        functools.partial(mix_kernel, start // LANES, tiles),
        in_specs=[SCALAR, WHOLE],
        out_specs=WHOLE,
        out_shape=jax.ShapeDtypeStruct((blocks, share, width), jnp.float32),
        scratch_shapes=[
            pltpu.VMEM((blocks, SUBLANES, LANES), jnp.int32),
            pltpu.VMEM((blocks, SUBLANES, LANES), jnp.float32),
        ],
    )(block, segments)


def product_kernel(group, offset, count, col_ref, *refs):
    parts = refs[:count]
    total_ref = refs[count] if offset else None
    last = offset + parts[0].shape[1] == group
    squares_ref = refs[-4] if last else None
    grads_ref, out_ref, terms_ref = refs[-3:]
    rows, width = parts[0].shape

    @pl.when(pl.program_id(0) == 0)
    def _():
        for shift in range(count):
            value = parts[shift][...]
            coarse = value.astype(jnp.bfloat16)
            at = slice(shift * width, (shift + 1) * width)
            terms_ref[:rows, at] = coarse
            terms_ref[rows:, at] = (value - coarse.astype(jnp.float32)).astype(jnp.bfloat16)

    both = None
    for shift in range(count):
        source = lax.rem(col_ref[0] + count - shift, count)
        at = pl.ds(pl.multiple_of(source * group + offset, LANES), width)
        step = jnp.dot(
            terms_ref[:, shift * width:(shift + 1) * width],
            grads_ref[at, :],
            preferred_element_type=jnp.float32,
        )
        both = step if both is None else both + step
    value = both[:rows] + both[rows:]
    if offset:
        value = value + total_ref[...]
    if last:
        squares = jnp.sum(squares_ref[...], axis=0)
        scale = lax.rsqrt(squares / D + epsilon)
        value = value * jnp.tile(scale, (1, value.shape[1] // LANES))
    out_ref[...] = value


def product(group, offset, col, parts, total, squares, grads):
    rows, width = parts[0].shape
    tokens, columns = grads.shape
    tile = 256
    column_tile = pl.BlockSpec((rows, tile), lambda i: (0, i))
    totals = [total] if offset else []
    norms = [squares] if offset + width == group else []
    return pl.pallas_call(
        functools.partial(product_kernel, group, offset, len(parts)),
        grid=(columns // tile,),
        in_specs=[
            SCALAR,
            *[WHOLE] * len(parts),
            *[column_tile] * len(totals),
            *[WHOLE] * len(norms),
            pl.BlockSpec((tokens, tile), lambda i: (0, i)),
        ],
        out_specs=column_tile,
        out_shape=jax.ShapeDtypeStruct((rows, columns), jnp.float32),
        scratch_shapes=[pltpu.VMEM((2 * rows, len(parts) * width), jnp.bfloat16)],
    )(col, *parts, *totals, *norms, grads)


def col_shift(value, shift):
    cols = lax.axis_size("cols")
    return lax.ppermute(value, "cols", [(c, (c + shift) % cols) for c in range(cols)])


def exchange(value):
    return lax.all_to_all(value, "rows", 0, 0, tiled=True)


def staged(hidden_acts, out_grads, row_signs, kept_index):
    row_devices = lax.axis_size("rows")
    cols = lax.axis_size("cols")
    block = lax.axis_index("rows")
    col = lax.axis_index("cols")[None]
    pad_rows = PADDED // row_devices
    own_rows, tokens = hidden_acts.shape[1:]
    share = kept_index.shape[0] // row_devices
    group = tokens // cols
    tiles = group // LANES
    grads = out_grads[0]

    table = jnp.asarray(sylvester(pad_rows)[:, :own_rows], dtype=jnp.bfloat16)
    segments = inner(
        col,
        table,
        row_signs[None],
        kept_index.reshape(-1, LANES),
        hidden_acts,
        row_devices,
        group,
    )
    segments = exchange(segments.reshape(row_devices, 1, -1)).reshape(-1, LANES)

    gradient = jnp.dot(hidden_acts[0], grads, preferred_element_type=jnp.float32)
    squares = jnp.sum(gradient * gradient)
    squares = jnp.broadcast_to(squares, (SUBLANES, LANES))
    for bit in (1, 2):
        squares = squares + lax.ppermute(
            squares, "cols", [(c, c ^ bit) for c in range(cols)]
        )
    squares = jnp.broadcast_to(squares[:1], (row_devices, 1, LANES))
    squares = exchange(squares)

    total, start = None, 0
    for width in CHUNKS:
        kept = mix(block[None], segments, row_devices, share, tiles, start, width)
        kept = exchange(kept)
        kept = kept.reshape(row_devices * share, width)
        parts = [kept]
        for shift in range(1, cols):
            parts.append(col_shift(kept, shift))
        total = product(group, start, col, parts, total, squares, grads)
        start += width
    return total[None]


def solution(mesh):
    return jax.shard_map(
        staged,
        mesh=mesh,
        in_specs=(P(None, "rows", None), P(None, None, "cols"), P("rows"), P("rows")),
        out_specs=P(None, "rows", "cols"),
        check_vma=False,
    )
```

```python
import functools

import jax
import jax.numpy as jnp
import numpy as np
from jax import lax
from jax.experimental import pallas as pl
from jax.experimental.pallas import tpu as pltpu
from jax.sharding import PartitionSpec as P


D = 5120
PADDED = 32768

epsilon = 1e-06


def sylvester(length):
    i = np.arange(length)
    common = i[:, None] & i[None, :]
    parity = np.zeros_like(common)
    for bit in range(length.bit_length() - 1):
        parity ^= common >> bit & 1
    return 1 - 2 * parity


LANES = 128
SUBLANES = 8
CHUNKS = (384, 256)

WHOLE = pl.BlockSpec(memory_space=pltpu.VMEM)
SCALAR = pl.BlockSpec(memory_space=pltpu.SMEM)


def resident(value):
    return pltpu.with_memory_space_constraint(value, pltpu.VMEM)


def butterfly(rows):
    count = len(rows)
    bit = 1
    while bit < count:
        rows = [
            rows[i ^ bit] - rows[i] if i & bit else rows[i] + rows[i ^ bit]
            for i in range(count)
        ]
        bit *= 2
    return rows


def inner_kernel(blocks, col_ref, table_ref, signs_ref, kept_ref, acts_ref, out_ref):
    tiles = acts_ref.shape[2] // LANES
    stride = tiles * SUBLANES + 1
    table = table_ref[...] * signs_ref[...].astype(jnp.float32).astype(jnp.bfloat16)
    mixed = jnp.dot(table, acts_ref[0], preferred_element_type=jnp.float32)
    kept = kept_ref[...].astype(jnp.float32)
    share = kept.size // blocks
    for block in range(blocks):
        rows = slice(block * SUBLANES, (block + 1) * SUBLANES)
        for tile in range(tiles):
            out_ref[pl.ds(block * stride + tile * SUBLANES, SUBLANES), :] = mixed[
                rows, tile * LANES:(tile + 1) * LANES
            ]
        row = block * share // LANES
        out_ref[pl.ds((block + 1) * stride - 1, 1), :] = kept[row:row + 1]


def inner(col, table, signs, kept, acts, blocks, width):
    own_rows = acts.shape[1]
    rows = blocks * (width // LANES * SUBLANES + 1)
    return pl.pallas_call(
        functools.partial(inner_kernel, blocks),
        grid_spec=pltpu.PrefetchScalarGridSpec(
            num_scalar_prefetch=1,
            grid=(1,),
            in_specs=[
                pl.BlockSpec(table.shape, lambda i, c: (0, 0)),
                pl.BlockSpec(signs.shape, lambda i, c: (0, 0)),
                pl.BlockSpec(kept.shape, lambda i, c: (0, 0)),
                pl.BlockSpec((1, own_rows, width), lambda i, c: (0, 0, c[0])),
            ],
            out_specs=pl.BlockSpec((rows, LANES), lambda i, c: (0, 0)),
        ),
        out_shape=jax.ShapeDtypeStruct((rows, LANES), jnp.float32),
    )(col, table, signs, kept, acts)


def mix_kernel(first, tiles, block_ref, segments_ref, kept_ref, position_ref, work_ref):
    blocks, share, width = kept_ref.shape
    low_count = blocks // 8
    stride = tiles * SUBLANES + 1

    sublane = lax.broadcasted_iota(jnp.int32, (SUBLANES, LANES), 0)
    lane = lax.rem(block_ref[0], LANES // share) * share + jnp.minimum(sublane, share - 1)
    for block in range(blocks):
        row = segments_ref[pl.ds((block + 1) * stride - 1, 1), :]
        row = jnp.broadcast_to(row, (SUBLANES, LANES)).astype(jnp.int32) & (SUBLANES - 1)
        position_ref[block] = jnp.take_along_axis(
            row, lane, axis=1, mode="promise_in_bounds"
        )

    for tile in range(width // LANES):
        at = slice(tile * LANES, (tile + 1) * LANES)
        for high in range(8):
            rows = butterfly(
                [
                    segments_ref[
                        pl.ds(
                            (high * low_count + low) * stride + (first + tile) * SUBLANES,
                            SUBLANES,
                        ),
                        :,
                    ]
                    for low in range(low_count)
                ]
            )
            for low in range(low_count):
                work_ref[high * low_count + low] = rows[low]
        for low in range(low_count):
            rows = butterfly([work_ref[high * low_count + low] for high in range(8)])
            for high in range(8):
                block = high * low_count + low
                picked = jnp.take_along_axis(
                    rows[high], position_ref[block], axis=0, mode="promise_in_bounds"
                )
                kept_ref[block, :, at] = picked[:share]


def mix(block, segments, blocks, share, tiles, start, width):
    return pl.pallas_call(
        functools.partial(mix_kernel, start // LANES, tiles),
        in_specs=[SCALAR, WHOLE],
        out_specs=WHOLE,
        out_shape=jax.ShapeDtypeStruct((blocks, share, width), jnp.float32),
        scratch_shapes=[
            pltpu.VMEM((blocks, SUBLANES, LANES), jnp.int32),
            pltpu.VMEM((blocks, SUBLANES, LANES), jnp.float32),
        ],
    )(block, resident(segments))


def product_kernel(group, offset, count, col_ref, *refs):
    parts = refs[:count]
    total_ref = refs[count] if offset else None
    last = offset + parts[0].shape[1] == group
    squares_ref = refs[-4] if last else None
    grads_ref, out_ref, terms_ref = refs[-3:]
    rows, width = parts[0].shape

    @pl.when(pl.program_id(0) == 0)
    def _():
        for shift in range(count):
            value = parts[shift][...]
            coarse = value.astype(jnp.bfloat16)
            at = slice(shift * width, (shift + 1) * width)
            terms_ref[:rows, at] = coarse
            terms_ref[rows:, at] = (value - coarse.astype(jnp.float32)).astype(jnp.bfloat16)

    both = None
    for shift in range(count):
        source = lax.rem(col_ref[0] + count - shift, count)
        at = pl.ds(pl.multiple_of(source * group + offset, LANES), width)
        step = jnp.dot(
            terms_ref[:, shift * width:(shift + 1) * width],
            grads_ref[at, :],
            preferred_element_type=jnp.float32,
        )
        both = step if both is None else both + step
    value = both[:rows] + both[rows:]
    if offset:
        value = value + total_ref[...]
    if last:
        squares = jnp.sum(squares_ref[...], axis=0)
        scale = lax.rsqrt(squares / D + epsilon)
        value = value * jnp.tile(scale, (1, value.shape[1] // LANES))
    out_ref[...] = value


def product(group, offset, col, parts, total, squares, grads):
    rows, width = parts[0].shape
    tokens, columns = grads.shape
    tile = 256
    column_tile = pl.BlockSpec((rows, tile), lambda i: (0, i))
    totals = [total] if offset else []
    norms = [squares] if offset + width == group else []
    return pl.pallas_call(
        functools.partial(product_kernel, group, offset, len(parts)),
        grid=(columns // tile,),
        in_specs=[
            SCALAR,
            *[WHOLE] * len(parts),
            *[column_tile] * len(totals),
            *[WHOLE] * len(norms),
            pl.BlockSpec((tokens, tile), lambda i: (0, i)),
        ],
        out_specs=column_tile,
        out_shape=jax.ShapeDtypeStruct((rows, columns), jnp.float32),
        scratch_shapes=[pltpu.VMEM((2 * rows, len(parts) * width), jnp.bfloat16)],
    )(col, *map(resident, parts), *totals, *map(resident, norms), grads)


def col_shift(value, shift):
    cols = lax.axis_size("cols")
    return lax.ppermute(value, "cols", [(c, (c + shift) % cols) for c in range(cols)])


def exchange(value):
    return lax.all_to_all(value, "rows", 0, 0, tiled=True)


def staged(hidden_acts, out_grads, row_signs, kept_index):
    row_devices = lax.axis_size("rows")
    cols = lax.axis_size("cols")
    block = lax.axis_index("rows")
    col = lax.axis_index("cols")[None]
    pad_rows = PADDED // row_devices
    own_rows, tokens = hidden_acts.shape[1:]
    share = kept_index.shape[0] // row_devices
    group = tokens // cols
    tiles = group // LANES
    grads = out_grads[0]

    table = jnp.asarray(sylvester(pad_rows)[:, :own_rows], dtype=jnp.bfloat16)
    segments = inner(
        col,
        table,
        row_signs[None],
        kept_index.reshape(-1, LANES),
        hidden_acts,
        row_devices,
        group,
    )
    segments = exchange(segments.reshape(row_devices, 1, -1)).reshape(-1, LANES)

    gradient = jnp.dot(hidden_acts[0], grads, preferred_element_type=jnp.float32)
    squares = jnp.sum(gradient * gradient)
    squares = jnp.broadcast_to(squares, (SUBLANES, LANES))
    for bit in (1, 2):
        squares = squares + lax.ppermute(
            squares, "cols", [(c, c ^ bit) for c in range(cols)]
        )
    squares = jnp.broadcast_to(squares[:1], (row_devices, 1, LANES))
    squares = exchange(squares)

    total, start = None, 0
    for width in CHUNKS:
        kept = mix(block[None], segments, row_devices, share, tiles, start, width)
        kept = exchange(kept)
        kept = kept.reshape(row_devices * share, width)
        parts = [kept]
        for shift in range(1, cols):
            parts.append(col_shift(kept, shift))
        total = product(group, start, col, parts, total, squares, grads)
        start += width
    return total[None]


def solution(mesh):
    return jax.shard_map(
        staged,
        mesh=mesh,
        in_specs=(P(None, "rows", None), P(None, None, "cols"), P("rows"), P("rows")),
        out_specs=P(None, "rows", "cols"),
        check_vma=False,
    )
```

```python
import functools

import jax
import jax.numpy as jnp
import numpy as np
from jax import lax
from jax.experimental import pallas as pl
from jax.experimental.pallas import tpu as pltpu
from jax.sharding import PartitionSpec as P


D = 5120
PADDED = 32768

epsilon = 1e-06


def sylvester(length):
    i = np.arange(length)
    common = i[:, None] & i[None, :]
    parity = np.zeros_like(common)
    for bit in range(length.bit_length() - 1):
        parity ^= common >> bit & 1
    return 1 - 2 * parity


LANES = 128
SUBLANES = 8

WHOLE = pl.BlockSpec(memory_space=pltpu.VMEM)
SCALAR = pl.BlockSpec(memory_space=pltpu.SMEM)


def resident(value):
    return pltpu.with_memory_space_constraint(value, pltpu.VMEM)


def butterfly(rows):
    count = len(rows)
    bit = 1
    while bit < count:
        rows = [
            rows[i ^ bit] - rows[i] if i & bit else rows[i] + rows[i ^ bit]
            for i in range(count)
        ]
        bit *= 2
    return rows


def inner_kernel(blocks, col_ref, table_ref, signs_ref, kept_ref, acts_ref, out_ref):
    tiles = acts_ref.shape[2] // LANES
    stride = tiles * SUBLANES + 1
    table = table_ref[...] * signs_ref[...].astype(jnp.float32).astype(jnp.bfloat16)
    mixed = jnp.dot(table, acts_ref[0], preferred_element_type=jnp.float32)
    kept = kept_ref[...].astype(jnp.float32)
    share = kept.size // blocks
    for block in range(blocks):
        rows = slice(block * SUBLANES, (block + 1) * SUBLANES)
        for tile in range(tiles):
            out_ref[pl.ds(block * stride + tile * SUBLANES, SUBLANES), :] = mixed[
                rows, tile * LANES:(tile + 1) * LANES
            ]
        row = block * share // LANES
        out_ref[pl.ds((block + 1) * stride - 1, 1), :] = kept[row:row + 1]


def inner(col, table, signs, kept, acts, blocks, width):
    own_rows = acts.shape[1]
    rows = blocks * (width // LANES * SUBLANES + 1)
    return pl.pallas_call(
        functools.partial(inner_kernel, blocks),
        grid_spec=pltpu.PrefetchScalarGridSpec(
            num_scalar_prefetch=1,
            grid=(1,),
            in_specs=[
                pl.BlockSpec(table.shape, lambda i, c: (0, 0)),
                pl.BlockSpec(signs.shape, lambda i, c: (0, 0)),
                pl.BlockSpec(kept.shape, lambda i, c: (0, 0)),
                pl.BlockSpec((1, own_rows, width), lambda i, c: (0, 0, c[0])),
            ],
            out_specs=pl.BlockSpec((rows, LANES), lambda i, c: (0, 0)),
        ),
        out_shape=jax.ShapeDtypeStruct((rows, LANES), jnp.float32),
    )(col, table, signs, kept, acts)


def mix_kernel(first, tiles, block_ref, segments_ref, kept_ref, position_ref, work_ref):
    blocks, share, width = kept_ref.shape
    low_count = blocks // 8
    stride = tiles * SUBLANES + 1

    sublane = lax.broadcasted_iota(jnp.int32, (SUBLANES, LANES), 0)
    lane = lax.rem(block_ref[0], LANES // share) * share + jnp.minimum(sublane, share - 1)
    for block in range(blocks):
        row = segments_ref[pl.ds((block + 1) * stride - 1, 1), :]
        row = jnp.broadcast_to(row, (SUBLANES, LANES)).astype(jnp.int32) & (SUBLANES - 1)
        position_ref[block] = jnp.take_along_axis(
            row, lane, axis=1, mode="promise_in_bounds"
        )

    for tile in range(width // LANES):
        at = slice(tile * LANES, (tile + 1) * LANES)
        for high in range(8):
            rows = butterfly(
                [
                    segments_ref[
                        pl.ds(
                            (high * low_count + low) * stride + (first + tile) * SUBLANES,
                            SUBLANES,
                        ),
                        :,
                    ]
                    for low in range(low_count)
                ]
            )
            for low in range(low_count):
                work_ref[high * low_count + low] = rows[low]
        for low in range(low_count):
            rows = butterfly([work_ref[high * low_count + low] for high in range(8)])
            for high in range(8):
                block = high * low_count + low
                picked = jnp.take_along_axis(
                    rows[high], position_ref[block], axis=0, mode="promise_in_bounds"
                )
                kept_ref[block, :, at] = picked[:share]


def mix(block, segments, blocks, share, tiles, start, width):
    return pl.pallas_call(
        functools.partial(mix_kernel, start // LANES, tiles),
        in_specs=[SCALAR, WHOLE],
        out_specs=WHOLE,
        out_shape=jax.ShapeDtypeStruct((blocks, share, width), jnp.float32),
        scratch_shapes=[
            pltpu.VMEM((blocks, SUBLANES, LANES), jnp.int32),
            pltpu.VMEM((blocks, SUBLANES, LANES), jnp.float32),
        ],
    )(block, resident(segments))


def product_kernel(shifts, adds, scales, col_ref, *refs):
    count = len(shifts)
    parts, refs = refs[:2 * count], refs[2 * count:]
    total_ref = refs[0] if adds else None
    squares_ref = refs[adds] if scales else None
    grads = refs[adds + scales:-2]
    out_ref, terms_ref = refs[-2:]
    half, width = parts[0].shape
    rows = 2 * half

    @pl.when(pl.program_id(0) == 0)
    def _():
        for i, part in enumerate(parts):
            value = part[...]
            coarse = value.astype(jnp.bfloat16)
            at = slice(i // 2 * width, (i // 2 + 1) * width)
            first = i % 2 * half
            terms_ref[first:first + half, at] = coarse
            terms_ref[rows + first:rows + first + half, at] = (
                value - coarse.astype(jnp.float32)
            ).astype(jnp.bfloat16)

    both = None
    for i in range(count):
        step = jnp.dot(
            terms_ref[:, i * width:(i + 1) * width],
            grads[i][...],
            preferred_element_type=jnp.float32,
        )
        both = step if both is None else both + step
    value = both[:rows] + both[rows:]
    if adds:
        value = value + total_ref[...]
    if scales:
        squares = jnp.sum(squares_ref[...], axis=0)
        scale = lax.rsqrt(squares / D + epsilon)
        value = value * jnp.tile(scale, (1, value.shape[1] // LANES))
    out_ref[...] = value


def product(col, parts, total, squares, grads):
    shifts = tuple(parts)
    halves = [resident(half) for shift in shifts for half in parts[shift]]
    half, width = halves[0].shape
    tokens, columns = grads.shape
    count = tokens // width
    tile = 256
    column_tile = pl.BlockSpec((2 * half, tile), lambda i, c: (0, i))
    totals = [] if total is None else [total]
    norms = [] if squares is None else [resident(squares)]

    def rows_of(shift):
        return pl.BlockSpec(
            (width, tile), lambda i, c: (lax.rem(c[0] + count - shift, count), i)
        )

    return pl.pallas_call(
        functools.partial(product_kernel, shifts, len(totals), len(norms)),
        grid_spec=pltpu.PrefetchScalarGridSpec(
            num_scalar_prefetch=1,
            grid=(columns // tile,),
            in_specs=[
                *[WHOLE] * len(halves),
                *[column_tile] * len(totals),
                *[WHOLE] * len(norms),
                *[rows_of(shift) for shift in shifts],
            ],
            out_specs=column_tile,
            scratch_shapes=[pltpu.VMEM((4 * half, len(shifts) * width), jnp.bfloat16)],
        ),
        out_shape=jax.ShapeDtypeStruct((2 * half, columns), jnp.float32),
    )(col, *halves, *totals, *norms, *[grads] * len(shifts))


def col_shift(value, shift):
    cols = lax.axis_size("cols")
    return lax.ppermute(value, "cols", [(c, (c + shift) % cols) for c in range(cols)])


def exchange(value):
    return lax.all_to_all(value, "rows", 0, 0, tiled=True)


def staged(hidden_acts, out_grads, row_signs, kept_index):
    row_devices = lax.axis_size("rows")
    cols = lax.axis_size("cols")
    block = lax.axis_index("rows")
    col = lax.axis_index("cols")[None]
    pad_rows = PADDED // row_devices
    own_rows, tokens = hidden_acts.shape[1:]
    share = kept_index.shape[0] // row_devices
    group = tokens // cols
    tiles = group // LANES
    grads = out_grads[0]

    table = jnp.asarray(sylvester(pad_rows)[:, :own_rows], dtype=jnp.bfloat16)
    segments = inner(
        col,
        table,
        row_signs[None],
        kept_index.reshape(-1, LANES),
        hidden_acts,
        row_devices,
        group,
    )
    segments = exchange(segments.reshape(row_devices, 1, -1)).reshape(-1, LANES)

    gradient = jnp.dot(hidden_acts[0], grads, preferred_element_type=jnp.float32)
    squares = jnp.sum(gradient * gradient)
    squares = jnp.broadcast_to(squares, (SUBLANES, LANES))
    for bit in (1, 2):
        squares = squares + lax.ppermute(
            squares, "cols", [(c, c ^ bit) for c in range(cols)]
        )
    squares = jnp.broadcast_to(squares[:1], (row_devices, 1, LANES))
    squares = exchange(squares)

    kept = mix(block[None], segments, row_devices, share, tiles, 0, group)
    kept = exchange(kept)

    half = row_devices // 2
    top = kept[:half].reshape(half * share, group)
    low = kept[half:].reshape(half * share, group)
    up_top = col_shift(top, 1)
    down_low = col_shift(low, -1)
    up_low = col_shift(low, 1)
    down_top = col_shift(top, -1)
    far_top = col_shift(up_top, 1)
    far_low = col_shift(down_low, -1)
    total = product(col, {0: (top, low)}, None, None, grads)
    total = product(col, {1: (up_top, up_low), cols - 1: (down_top, down_low)}, total, None, grads)
    total = product(col, {2: (far_top, far_low)}, total, squares, grads)
    return total[None]


def solution(mesh):
    return jax.shard_map(
        staged,
        mesh=mesh,
        in_specs=(P(None, "rows", None), P(None, None, "cols"), P("rows"), P("rows")),
        out_specs=P(None, "rows", "cols"),
        check_vma=False,
    )
```

```python
import functools

import jax
import jax.numpy as jnp
import numpy as np
from jax import lax
from jax.experimental import pallas as pl
from jax.experimental.pallas import tpu as pltpu
from jax.sharding import PartitionSpec as P


D = 5120
PADDED = 32768

epsilon = 1e-06


def sylvester(length):
    i = np.arange(length)
    common = i[:, None] & i[None, :]
    parity = np.zeros_like(common)
    for bit in range(length.bit_length() - 1):
        parity ^= common >> bit & 1
    return 1 - 2 * parity


LANES = 128
SUBLANES = 8

WHOLE = pl.BlockSpec(memory_space=pltpu.VMEM)
SCALAR = pl.BlockSpec(memory_space=pltpu.SMEM)
PARAMS = pltpu.CompilerParams(vmem_limit_bytes=24 * 2**20)


def resident(value):
    return pltpu.with_memory_space_constraint(value, pltpu.VMEM)


def butterfly(rows):
    count = len(rows)
    bit = 1
    while bit < count:
        rows = [
            rows[i ^ bit] - rows[i] if i & bit else rows[i] + rows[i ^ bit]
            for i in range(count)
        ]
        bit *= 2
    return rows


def inner_kernel(blocks, col_ref, table_ref, signs_ref, kept_ref, acts_ref, out_ref):
    tiles = acts_ref.shape[2] // LANES
    stride = tiles * SUBLANES + 1
    table = table_ref[...] * signs_ref[...].astype(jnp.float32).astype(jnp.bfloat16)
    mixed = jnp.dot(table, acts_ref[0], preferred_element_type=jnp.float32)
    kept = kept_ref[...].astype(jnp.float32)
    share = kept.size // blocks
    for block in range(blocks):
        rows = slice(block * SUBLANES, (block + 1) * SUBLANES)
        for tile in range(tiles):
            out_ref[pl.ds(block * stride + tile * SUBLANES, SUBLANES), :] = mixed[
                rows, tile * LANES:(tile + 1) * LANES
            ]
        row = block * share // LANES
        out_ref[pl.ds((block + 1) * stride - 1, 1), :] = kept[row:row + 1]


def inner(col, table, signs, kept, acts, blocks, width):
    own_rows = acts.shape[1]
    rows = blocks * (width // LANES * SUBLANES + 1)
    return pl.pallas_call(
        functools.partial(inner_kernel, blocks),
        grid_spec=pltpu.PrefetchScalarGridSpec(
            num_scalar_prefetch=1,
            grid=(1,),
            in_specs=[
                pl.BlockSpec(table.shape, lambda i, c: (0, 0)),
                pl.BlockSpec(signs.shape, lambda i, c: (0, 0)),
                pl.BlockSpec(kept.shape, lambda i, c: (0, 0)),
                pl.BlockSpec((1, own_rows, width), lambda i, c: (0, 0, c[0])),
            ],
            out_specs=WHOLE,
        ),
        out_shape=pltpu.VMEM((rows, LANES), jnp.float32),
        compiler_params=PARAMS,
    )(col, *[pltpu.with_memory_space_constraint(v, pltpu.HBM) for v in (table, signs, kept, acts)])


def mix_kernel(first, tiles, block_ref, segments_ref, kept_ref, position_ref, work_ref):
    blocks, share, width = kept_ref.shape
    low_count = blocks // 8
    stride = tiles * SUBLANES + 1

    sublane = lax.broadcasted_iota(jnp.int32, (SUBLANES, LANES), 0)
    lane = lax.rem(block_ref[0], LANES // share) * share + jnp.minimum(sublane, share - 1)
    for block in range(blocks):
        row = segments_ref[pl.ds((block + 1) * stride - 1, 1), :]
        row = jnp.broadcast_to(row, (SUBLANES, LANES)).astype(jnp.int32) & (SUBLANES - 1)
        position_ref[block] = jnp.take_along_axis(
            row, lane, axis=1, mode="promise_in_bounds"
        )

    for tile in range(width // LANES):
        at = slice(tile * LANES, (tile + 1) * LANES)
        for high in range(8):
            rows = butterfly(
                [
                    segments_ref[
                        pl.ds(
                            (high * low_count + low) * stride + (first + tile) * SUBLANES,
                            SUBLANES,
                        ),
                        :,
                    ]
                    for low in range(low_count)
                ]
            )
            for low in range(low_count):
                work_ref[high * low_count + low] = rows[low]
        for low in range(low_count):
            rows = butterfly([work_ref[high * low_count + low] for high in range(8)])
            for high in range(8):
                block = high * low_count + low
                picked = jnp.take_along_axis(
                    rows[high], position_ref[block], axis=0, mode="promise_in_bounds"
                )
                kept_ref[block, :, at] = picked[:share]


def mix(block, segments, blocks, share, tiles, start, width):
    return pl.pallas_call(
        functools.partial(mix_kernel, start // LANES, tiles),
        in_specs=[SCALAR, WHOLE],
        out_specs=WHOLE,
        out_shape=pltpu.VMEM((blocks, share, width), jnp.float32),
        compiler_params=PARAMS,
        scratch_shapes=[
            pltpu.VMEM((blocks, SUBLANES, LANES), jnp.int32),
            pltpu.VMEM((blocks, SUBLANES, LANES), jnp.float32),
        ],
    )(block, resident(segments))


def product_kernel(shifts, adds, scales, col_ref, *refs):
    count = len(shifts)
    parts, refs = refs[:2 * count], refs[2 * count:]
    total_ref = refs[0] if adds else None
    squares_ref = refs[adds] if scales else None
    grads_ref, out_ref, terms_ref, rows_ref, rows_sems = refs[adds + scales:adds + scales + 5]
    half, width = parts[0].shape
    rows = 2 * half
    columns = grads_ref.shape[1]
    groups = grads_ref.shape[0] // width
    tile = 256
    tiles = [slice(first, first + tile) for first in range(0, columns, tile)]

    fetches = []
    for index, at in enumerate(tiles):
        for i, shift in enumerate(shifts):
            source = lax.rem(col_ref[0] + groups - shift, groups)
            fetches.append(
                pltpu.make_async_copy(
                    grads_ref.at[pl.ds(pl.multiple_of(source * width, LANES), width), at],
                    rows_ref.at[i * width:(i + 1) * width, at],
                    rows_sems.at[index * count + i],
                )
            )
            fetches[-1].start()

    for i, part in enumerate(parts):
        value = part[...]
        coarse = value.astype(jnp.bfloat16)
        at = slice(i // 2 * width, (i // 2 + 1) * width)
        first = i % 2 * half
        terms_ref[first:first + half, at] = coarse
        terms_ref[rows + first:rows + first + half, at] = (
            value - coarse.astype(jnp.float32)
        ).astype(jnp.bfloat16)

    if scales:
        done_ref, sems = refs[-2:]
        squares = jnp.sum(squares_ref[...], axis=0)
        scale = jnp.tile(lax.rsqrt(squares / D + epsilon), (1, tile // LANES))
    copies = []
    for index, at in enumerate(tiles):
        for fetch in fetches[index * count:(index + 1) * count]:
            fetch.wait()
        both = jnp.dot(terms_ref[...], rows_ref[:, at], preferred_element_type=jnp.float32)
        value = both[:rows] + both[rows:]
        if adds:
            value = value + total_ref[:, at]
        if not scales:
            out_ref[:, at] = value
            continue
        done_ref[:, at] = value * scale
        copies.append(pltpu.make_async_copy(done_ref.at[:, at], out_ref.at[:, at], sems.at[index]))
        copies[-1].start()
    for copy in copies:
        copy.wait()


def product(col, parts, total, squares, grads):
    shifts = tuple(parts)
    halves = [half for shift in shifts for half in parts[shift]]
    half, width = halves[0].shape
    columns = grads.shape[1]
    operands = [*halves, *([] if total is None else [total]), *([] if squares is None else [squares])]
    last = squares is not None
    shape = (2 * half, columns)
    depth = len(shifts) * width
    scratch = [
        pltpu.VMEM((4 * half, depth), jnp.bfloat16),
        pltpu.VMEM((depth, columns), jnp.bfloat16),
        pltpu.SemaphoreType.DMA((len(shifts) * columns // 256,)),
    ]
    if last:
        scratch += [pltpu.VMEM(shape, jnp.float32), pltpu.SemaphoreType.DMA((columns // 256,))]
    return pl.pallas_call(
        functools.partial(product_kernel, shifts, int(total is not None), int(last)),
        in_specs=[SCALAR, *[WHOLE] * len(operands), pl.BlockSpec(memory_space=pl.ANY)],
        out_specs=pl.BlockSpec(memory_space=pl.ANY) if last else WHOLE,
        out_shape=jax.ShapeDtypeStruct(shape, jnp.float32) if last else pltpu.VMEM(shape, jnp.float32),
        scratch_shapes=scratch,
        compiler_params=PARAMS,
    )(col, *map(resident, operands), pltpu.with_memory_space_constraint(grads, pltpu.HBM))


def col_shift(value, shift):
    cols = lax.axis_size("cols")
    return lax.ppermute(value, "cols", [(c, (c + shift) % cols) for c in range(cols)])


def exchange(value):
    return lax.all_to_all(value, "rows", 0, 0, tiled=True)


def staged(hidden_acts, out_grads, row_signs, kept_index):
    row_devices = lax.axis_size("rows")
    cols = lax.axis_size("cols")
    block = lax.axis_index("rows")
    col = lax.axis_index("cols")[None]
    pad_rows = PADDED // row_devices
    own_rows, tokens = hidden_acts.shape[1:]
    share = kept_index.shape[0] // row_devices
    group = tokens // cols
    tiles = group // LANES
    grads = out_grads[0]

    table = jnp.asarray(sylvester(pad_rows)[:, :own_rows], dtype=jnp.bfloat16)
    segments = inner(
        col,
        table,
        row_signs[None],
        kept_index.reshape(-1, LANES),
        hidden_acts,
        row_devices,
        group,
    )
    segments = exchange(segments.reshape(row_devices, 1, -1)).reshape(-1, LANES)

    gradient = jnp.dot(hidden_acts[0], grads, preferred_element_type=jnp.float32)
    squares = jnp.sum(gradient * gradient)
    squares = jnp.broadcast_to(squares, (SUBLANES, LANES))
    for bit in (1, 2):
        squares = squares + lax.ppermute(
            squares, "cols", [(c, c ^ bit) for c in range(cols)]
        )
    squares = jnp.broadcast_to(squares[:1], (row_devices, 1, LANES))
    squares = exchange(squares)

    kept = mix(block[None], segments, row_devices, share, tiles, 0, group)
    kept = exchange(kept)

    half = row_devices // 2
    top = kept[:half].reshape(half * share, group)
    low = kept[half:].reshape(half * share, group)
    up_top = col_shift(top, 1)
    down_low = col_shift(low, -1)
    up_low = col_shift(low, 1)
    down_top = col_shift(top, -1)
    far_top = col_shift(up_top, 1)
    far_low = col_shift(down_low, -1)
    total = product(col, {0: (top, low)}, None, None, grads)
    total = product(col, {1: (up_top, up_low), cols - 1: (down_top, down_low)}, total, None, grads)
    total = product(col, {2: (far_top, far_low)}, total, squares, grads)
    return total[None]


def solution(mesh):
    return jax.shard_map(
        staged,
        mesh=mesh,
        in_specs=(P(None, "rows", None), P(None, None, "cols"), P("rows"), P("rows")),
        out_specs=P(None, "rows", "cols"),
        check_vma=False,
    )
```

```python
import functools

import jax
import jax.numpy as jnp
import numpy as np
from jax import lax
from jax.experimental import pallas as pl
from jax.experimental.pallas import tpu as pltpu
from jax.sharding import PartitionSpec as P


D = 5120
PADDED = 32768

epsilon = 1e-06


def sylvester(length):
    i = np.arange(length)
    common = i[:, None] & i[None, :]
    parity = np.zeros_like(common)
    for bit in range(length.bit_length() - 1):
        parity ^= common >> bit & 1
    return 1 - 2 * parity


LANES = 128
SUBLANES = 8

WHOLE = pl.BlockSpec(memory_space=pltpu.VMEM)
SCALAR = pl.BlockSpec(memory_space=pltpu.SMEM)
PARAMS = pltpu.CompilerParams(vmem_limit_bytes=24 * 2**20)


def resident(value):
    return pltpu.with_memory_space_constraint(value, pltpu.VMEM)


def butterfly(rows):
    count = len(rows)
    bit = 1
    while bit < count:
        rows = [
            rows[i ^ bit] - rows[i] if i & bit else rows[i] + rows[i ^ bit]
            for i in range(count)
        ]
        bit *= 2
    return rows


def inner_kernel(blocks, col_ref, table_ref, signs_ref, kept_ref, acts_ref, out_ref):
    tiles = acts_ref.shape[2] // LANES
    own_rows = acts_ref.shape[1]
    stride = tiles * SUBLANES + 1
    signs = signs_ref[...].astype(jnp.float32).astype(jnp.bfloat16)
    size = table_ref.shape[0]
    halves = butterfly(
        [
            jnp.dot(
                table_ref[:, :min(own_rows - first, size)] * signs[:, first:first + size],
                acts_ref[0, first:first + size],
                preferred_element_type=jnp.float32,
            )
            for first in (0, size)
        ]
    )
    kept = kept_ref[...].astype(jnp.float32)
    share = kept.size // blocks
    for block in range(blocks):
        half, first = divmod(block * SUBLANES, size)
        for tile in range(tiles):
            out_ref[pl.ds(block * stride + tile * SUBLANES, SUBLANES), :] = halves[half][
                first:first + SUBLANES, tile * LANES:(tile + 1) * LANES
            ]
        row = block * share // LANES
        out_ref[pl.ds((block + 1) * stride - 1, 1), :] = kept[row:row + 1]


def inner(col, table, signs, kept, acts, blocks, width):
    own_rows = acts.shape[1]
    rows = blocks * (width // LANES * SUBLANES + 1)
    return pl.pallas_call(
        functools.partial(inner_kernel, blocks),
        grid_spec=pltpu.PrefetchScalarGridSpec(
            num_scalar_prefetch=1,
            grid=(1,),
            in_specs=[
                pl.BlockSpec(table.shape, lambda i, c: (0, 0)),
                pl.BlockSpec(signs.shape, lambda i, c: (0, 0)),
                pl.BlockSpec(kept.shape, lambda i, c: (0, 0)),
                pl.BlockSpec((1, own_rows, width), lambda i, c: (0, 0, c[0])),
            ],
            out_specs=WHOLE,
        ),
        out_shape=pltpu.VMEM((rows, LANES), jnp.float32),
        compiler_params=PARAMS,
    )(col, *[pltpu.with_memory_space_constraint(v, pltpu.HBM) for v in (table, signs, kept, acts)])


def mix_kernel(first, tiles, block_ref, segments_ref, kept_ref, position_ref, work_ref):
    blocks, share, width = kept_ref.shape
    low_count = blocks // 8
    stride = tiles * SUBLANES + 1

    sublane = lax.broadcasted_iota(jnp.int32, (SUBLANES, LANES), 0)
    lane = lax.rem(block_ref[0], LANES // share) * share + jnp.minimum(sublane, share - 1)
    for block in range(blocks):
        row = segments_ref[pl.ds((block + 1) * stride - 1, 1), :]
        row = jnp.broadcast_to(row, (SUBLANES, LANES)).astype(jnp.int32) & (SUBLANES - 1)
        position_ref[block] = jnp.take_along_axis(
            row, lane, axis=1, mode="promise_in_bounds"
        )

    for tile in range(width // LANES):
        at = slice(tile * LANES, (tile + 1) * LANES)
        for high in range(8):
            rows = butterfly(
                [
                    segments_ref[
                        pl.ds(
                            (high * low_count + low) * stride + (first + tile) * SUBLANES,
                            SUBLANES,
                        ),
                        :,
                    ]
                    for low in range(low_count)
                ]
            )
            for low in range(low_count):
                work_ref[high * low_count + low] = rows[low]
        for low in range(low_count):
            rows = butterfly([work_ref[high * low_count + low] for high in range(8)])
            for high in range(8):
                block = high * low_count + low
                picked = jnp.take_along_axis(
                    rows[high], position_ref[block], axis=0, mode="promise_in_bounds"
                )
                kept_ref[block, :, at] = picked[:share]


def mix(block, segments, blocks, share, tiles, start, width):
    return pl.pallas_call(
        functools.partial(mix_kernel, start // LANES, tiles),
        in_specs=[SCALAR, WHOLE],
        out_specs=WHOLE,
        out_shape=pltpu.VMEM((blocks, share, width), jnp.float32),
        compiler_params=PARAMS,
        scratch_shapes=[
            pltpu.VMEM((blocks, SUBLANES, LANES), jnp.int32),
            pltpu.VMEM((blocks, SUBLANES, LANES), jnp.float32),
        ],
    )(block, resident(segments))


def product_kernel(shifts, adds, scales, ahead, col_ref, *refs):
    count = len(shifts)
    parts, refs = refs[:2 * count], refs[2 * count:]
    total_ref, refs = (refs[0], refs[1:]) if adds else (None, refs)
    squares, refs = (refs[:2], refs[2:]) if scales else (None, refs)
    grads_ref, refs = refs[0], refs[1:]
    if scales:
        out_ref, terms_ref, done_ref, sems = refs
        rows_ref = grads_ref
    else:
        ahead_ref, refs = (refs[1], refs[:1] + refs[2:]) if ahead else (None, refs)
        out_ref, terms_ref, rows_ref, rows_sems = refs
    half, width = parts[0].shape
    rows = 2 * half
    columns = grads_ref.shape[1]
    tile = 256
    tiles = [slice(first, first + tile) for first in range(0, columns, tile)]

    def fetch(shift, at, out, sem):
        groups = grads_ref.shape[0] // width
        source = lax.rem(col_ref[0] + groups - shift, groups)
        copy = pltpu.make_async_copy(
            grads_ref.at[pl.ds(pl.multiple_of(source * width, LANES), width), at], out, sem
        )
        copy.start()
        return copy

    fetches = [
        fetch(
            shift,
            at,
            rows_ref.at[i * width:(i + 1) * width, at],
            rows_sems.at[index * count + i],
        )
        for index, at in enumerate(tiles)
        for i, shift in enumerate(shifts)
        if not scales
    ]
    if ahead:
        later = fetch(ahead, slice(None), ahead_ref, rows_sems.at[len(fetches)])

    for i, part in enumerate(parts):
        value = part[...]
        coarse = value.astype(jnp.bfloat16)
        at = slice(i // 2 * width, (i // 2 + 1) * width)
        first = i % 2 * half
        terms_ref[first:first + half, at] = coarse
        terms_ref[rows + first:rows + first + half, at] = (
            value - coarse.astype(jnp.float32)
        ).astype(jnp.bfloat16)

    if scales:
        squares = squares[0][:1] + squares[1][:1]
        scale = jnp.tile(lax.rsqrt(squares / D + epsilon), (1, tile // LANES))
    copies = []
    for index, at in enumerate(tiles):
        for copy in fetches[index * count:(index + 1) * count]:
            copy.wait()
        both = jnp.dot(terms_ref[...], rows_ref[:, at], preferred_element_type=jnp.float32)
        value = both[:rows] + both[rows:]
        if adds:
            value = value + total_ref[:, at]
        if not scales:
            out_ref[:, at] = value
            continue
        done_ref[:, at] = value * scale
        copies.append(pltpu.make_async_copy(done_ref.at[:, at], out_ref.at[:, at], sems.at[index]))
        copies[-1].start()
    for copy in copies:
        copy.wait()
    if ahead:
        later.wait()


def product(col, parts, grads, total=None, squares=None, ahead=None):
    shifts = tuple(parts)
    last = squares is not None
    halves = [half for shift in shifts for half in parts[shift]]
    half, width = halves[0].shape
    columns = grads.shape[1]
    depth = len(shifts) * width
    operands = [*halves, *([] if total is None else [total]), *(squares or ())]
    shape = (2 * half, columns)
    anywhere = pl.BlockSpec(memory_space=pl.ANY)
    scratch = [pltpu.VMEM((4 * half, depth), jnp.bfloat16)]
    if last:
        grads = resident(grads)
        outs, specs = jax.ShapeDtypeStruct(shape, jnp.float32), anywhere
        scratch += [
            pltpu.VMEM(shape, jnp.float32),
            pltpu.SemaphoreType.DMA((columns // 256,)),
        ]
    else:
        grads = pltpu.with_memory_space_constraint(grads, pltpu.HBM)
        outs, specs = [pltpu.VMEM(shape, jnp.float32)], [WHOLE]
        if ahead:
            outs.append(pltpu.VMEM((width, columns), grads.dtype))
            specs.append(WHOLE)
        scratch += [
            pltpu.VMEM((depth, columns), jnp.bfloat16),
            pltpu.SemaphoreType.DMA((len(shifts) * columns // 256 + 1,)),
        ]
    return pl.pallas_call(
        functools.partial(product_kernel, shifts, total is not None, last, ahead),
        in_specs=[SCALAR, *[WHOLE] * len(operands), WHOLE if last else anywhere],
        out_specs=specs,
        out_shape=outs,
        scratch_shapes=scratch,
        compiler_params=PARAMS,
    )(col, *map(resident, operands), grads)


def col_shift(value, shift):
    cols = lax.axis_size("cols")
    return lax.ppermute(value, "cols", [(c, (c + shift) % cols) for c in range(cols)])


def exchange(value):
    return lax.all_to_all(value, "rows", 0, 0, tiled=True)


def staged(hidden_acts, out_grads, row_signs, kept_index):
    row_devices = lax.axis_size("rows")
    cols = lax.axis_size("cols")
    block = lax.axis_index("rows")
    col = lax.axis_index("cols")[None]
    pad_rows = PADDED // row_devices
    _, tokens = hidden_acts.shape[1:]
    share = kept_index.shape[0] // row_devices
    group = tokens // cols
    tiles = group // LANES
    grads = out_grads[0]

    table = jnp.asarray(sylvester(pad_rows // 2), dtype=jnp.bfloat16)
    segments = inner(
        col,
        table,
        row_signs[None],
        kept_index.reshape(-1, LANES),
        hidden_acts,
        row_devices,
        group,
    )
    segments = exchange(segments.reshape(row_devices, 1, -1)).reshape(-1, LANES)

    gradient = jnp.dot(hidden_acts[0], grads, preferred_element_type=jnp.float32)
    squares = jnp.sum(gradient * gradient)
    squares = jnp.broadcast_to(squares, (SUBLANES, LANES))
    steps = [("y", 1, "cols"), ("y", 2, "cols"), ("c", 1, "rows"), ("x", 16, "rows")]
    steps += [("x", 32, "rows"), ("z", 2, "rows"), ("z", 4, "rows"), ("z", 8, "rows")]
    for name, mask, axis in steps:
        other = lax.ppermute(
            squares, axis, [(i, i ^ mask) for i in range(lax.axis_size(axis))]
        )
        if (name, mask) != steps[-1][:2]:
            squares = squares + other

    kept = mix(block[None], segments, row_devices, share, tiles, 0, group)
    kept = exchange(kept)

    half = row_devices // 2
    top = kept[:half].reshape(half * share, group)
    low = kept[half:].reshape(half * share, group)
    up_top = col_shift(top, 1)
    down_low = col_shift(low, -1)
    up_low = col_shift(low, 1)
    down_top = col_shift(top, -1)
    far_top = col_shift(up_top, 1)
    far_low = col_shift(down_low, -1)
    (total,) = product(col, {0: (top, low)}, grads)
    parts = {1: (up_top, up_low), cols - 1: (down_top, down_low)}
    total, rows = product(col, parts, grads, total, ahead=2)
    total = product(col, {2: (far_top, far_low)}, rows, total, (squares, other))
    return total[None]


def solution(mesh):
    return jax.shard_map(
        staged,
        mesh=mesh,
        in_specs=(P(None, "rows", None), P(None, None, "cols"), P("rows"), P("rows")),
        out_specs=P(None, "rows", "cols"),
        check_vma=False,
    )
```

```python
import functools

import jax
import jax.numpy as jnp
import numpy as np
from jax import lax
from jax.experimental import pallas as pl
from jax.experimental.pallas import tpu as pltpu
from jax.sharding import PartitionSpec as P


D = 5120
PADDED = 32768

epsilon = 1e-06


def sylvester(length):
    i = np.arange(length)
    common = i[:, None] & i[None, :]
    parity = np.zeros_like(common)
    for bit in range(length.bit_length() - 1):
        parity ^= common >> bit & 1
    return 1 - 2 * parity


LANES = 128
SUBLANES = 8

WHOLE = pl.BlockSpec(memory_space=pltpu.VMEM)
SCALAR = pl.BlockSpec(memory_space=pltpu.SMEM)
PARAMS = pltpu.CompilerParams(vmem_limit_bytes=24 * 2**20)


def resident(value):
    return pltpu.with_memory_space_constraint(value, pltpu.VMEM)


def butterfly(rows):
    count = len(rows)
    bit = 1
    while bit < count:
        rows = [
            rows[i ^ bit] - rows[i] if i & bit else rows[i] + rows[i ^ bit]
            for i in range(count)
        ]
        bit *= 2
    return rows


def inner_kernel(blocks, col_ref, table_ref, signs_ref, kept_ref, acts_ref, out_ref):
    tiles = acts_ref.shape[2] // LANES
    own_rows = acts_ref.shape[1]
    stride = tiles * SUBLANES + 1
    signs = signs_ref[...].astype(jnp.float32).astype(jnp.bfloat16)
    size = table_ref.shape[0]
    halves = butterfly(
        [
            jnp.dot(
                table_ref[:, :min(own_rows - first, size)] * signs[:, first:first + size],
                acts_ref[0, first:first + size],
                preferred_element_type=jnp.float32,
            )
            for first in (0, size)
        ]
    )
    kept = kept_ref[...].astype(jnp.float32)
    share = kept.size // blocks
    for block in range(blocks):
        segment = block % 2 * (blocks // 2) + block // 2
        half, first = divmod(segment * SUBLANES, size)
        for tile in range(tiles):
            out_ref[pl.ds(block * stride + tile * SUBLANES, SUBLANES), :] = halves[half][
                first:first + SUBLANES, tile * LANES:(tile + 1) * LANES
            ]
        row = segment * share // LANES
        out_ref[pl.ds((block + 1) * stride - 1, 1), :] = kept[row:row + 1]


def inner(col, table, signs, kept, acts, blocks, width):
    own_rows = acts.shape[1]
    rows = blocks * (width // LANES * SUBLANES + 1)
    return pl.pallas_call(
        functools.partial(inner_kernel, blocks),
        grid_spec=pltpu.PrefetchScalarGridSpec(
            num_scalar_prefetch=1,
            grid=(1,),
            in_specs=[
                pl.BlockSpec(table.shape, lambda i, c: (0, 0)),
                pl.BlockSpec(signs.shape, lambda i, c: (0, 0)),
                pl.BlockSpec(kept.shape, lambda i, c: (0, 0)),
                pl.BlockSpec((1, own_rows, width), lambda i, c: (0, 0, c[0])),
            ],
            out_specs=WHOLE,
        ),
        out_shape=pltpu.VMEM((rows, LANES), jnp.float32),
        compiler_params=PARAMS,
    )(col, *[pltpu.with_memory_space_constraint(v, pltpu.HBM) for v in (table, signs, kept, acts)])


def mix_kernel(first, tiles, block_ref, segments_ref, kept_ref, position_ref, work_ref):
    pairs, _, width = kept_ref.shape
    blocks, share = 2 * pairs, SUBLANES // 2
    low_count = blocks // 8
    stride = tiles * SUBLANES + 1

    sublane = lax.broadcasted_iota(jnp.int32, (SUBLANES, LANES), 0)
    lane = block_ref[0] // 2 * share + lax.rem(sublane, share)
    even = (sublane < share) == (lax.rem(block_ref[0], 2) == 0)
    for block in range(blocks):
        row = segments_ref[pl.ds((block + 1) * stride - 1, 1), :]
        row = jnp.broadcast_to(row, (SUBLANES, LANES)).astype(jnp.int32) & (SUBLANES - 1)
        position_ref[block] = jnp.take_along_axis(
            row, lane, axis=1, mode="promise_in_bounds"
        )

    for tile in range(width // LANES):
        at = slice(tile * LANES, (tile + 1) * LANES)
        for high in range(8):
            rows = butterfly(
                [
                    segments_ref[
                        pl.ds(
                            (high * low_count + low) * stride + (first + tile) * SUBLANES,
                            SUBLANES,
                        ),
                        :,
                    ]
                    for low in range(low_count)
                ]
            )
            for low in range(low_count):
                work_ref[high * low_count + low] = rows[low]
        for low in range(low_count):
            rows = butterfly([work_ref[high * low_count + low] for high in range(8)])
            for high in range(8):
                work_ref[high * low_count + low] = rows[high]
        for pair in range(pairs):
            low_block, high_block = [
                jnp.take_along_axis(
                    work_ref[block], position_ref[block], axis=0, mode="promise_in_bounds"
                )
                for block in (2 * pair, 2 * pair + 1)
            ]
            kept_ref[pair, :, at] = jnp.where(even, low_block, high_block)


def mix(block, segments, blocks, share, tiles, start, width):
    return pl.pallas_call(
        functools.partial(mix_kernel, start // LANES, tiles),
        in_specs=[SCALAR, WHOLE],
        out_specs=WHOLE,
        out_shape=pltpu.VMEM((blocks // 2, 2 * share, width), jnp.float32),
        compiler_params=PARAMS,
        scratch_shapes=[
            pltpu.VMEM((blocks, SUBLANES, LANES), jnp.int32),
            pltpu.VMEM((blocks, SUBLANES, LANES), jnp.float32),
        ],
    )(block, resident(segments))


def product_kernel(shifts, pieces, adds, scales, ahead, col_ref, core_ref, *refs):
    count = len(shifts)
    parts, refs = refs[:pieces * count], refs[pieces * count:]
    total_ref, refs = (refs[0], refs[1:]) if adds else (None, refs)
    squares, refs = (refs[:2], refs[2:]) if scales else (None, refs)
    grads_ref, refs = refs[0], refs[1:]
    if scales:
        out_ref, terms_ref, done_ref, sems = refs
        rows_ref = grads_ref
    else:
        ahead_ref, refs = (refs[1], refs[:1] + refs[2:]) if ahead else (None, refs)
        out_ref, terms_ref, rows_ref, rows_sems = refs
    piece, width = parts[0].shape
    rows = pieces * piece
    half = rows // 2
    columns = grads_ref.shape[1]
    tile = 256 if scales else columns
    tiles = [slice(first, first + tile) for first in range(0, columns, tile)]

    def fetch(shift, at, out, sem):
        groups = grads_ref.shape[0] // width
        source = lax.rem(col_ref[0] + groups - shift, groups)
        copy = pltpu.make_async_copy(
            grads_ref.at[pl.ds(pl.multiple_of(source * width, LANES), width), at], out, sem
        )
        copy.start()
        return copy

    fetches = [
        fetch(
            shift,
            at,
            rows_ref.at[i * width:(i + 1) * width, at],
            rows_sems.at[index * count + i],
        )
        for index, at in enumerate(tiles)
        for i, shift in enumerate(shifts)
        if not scales
    ]
    if ahead:
        later = fetch(ahead, slice(None), ahead_ref, rows_sems.at[len(fetches)])

    for i, part in enumerate(parts):
        value = part[...]
        coarse = value.astype(jnp.bfloat16)
        at = slice(i // pieces * width, (i // pieces + 1) * width)
        first = i % pieces * piece
        terms_ref[first:first + piece, at] = coarse
        terms_ref[rows + first:rows + first + piece, at] = (
            value - coarse.astype(jnp.float32)
        ).astype(jnp.bfloat16)

    if scales:
        squares = squares[0][:1] + squares[1][:1]
        scale = jnp.tile(lax.rsqrt(squares / D + epsilon), (1, tile // LANES))
    copies = []
    for index, at in enumerate(tiles):
        for copy in fetches[index * count:(index + 1) * count]:
            copy.wait()
        both = jnp.dot(terms_ref[...], rows_ref[:, at], preferred_element_type=jnp.float32)
        value = both[:rows] + both[rows:]
        if adds:
            value = value + total_ref[:, at]
        if not scales:
            out_ref[:, at] = value
            continue
        done_ref[:, at] = value * scale
        for i in range(2):
            first = pl.multiple_of(lax.rem(core_ref[0] + i, 2) * half, half)
            copies.append(
                pltpu.make_async_copy(
                    done_ref.at[i * half:(i + 1) * half, at],
                    out_ref.at[pl.ds(first, half), at],
                    sems.at[index, i],
                )
            )
            copies[-1].start()
    for copy in copies:
        copy.wait()
    if ahead:
        later.wait()


def product(col, core, parts, grads, total=None, squares=None, ahead=None):
    shifts = tuple(parts)
    last = squares is not None
    halves = [half for shift in shifts for half in parts[shift]]
    piece, width = halves[0].shape
    pieces = len(halves) // len(shifts)
    rows = pieces * piece
    columns = grads.shape[1]
    depth = len(shifts) * width
    operands = [*halves, *([] if total is None else [total]), *(squares or ())]
    shape = (rows, columns)
    anywhere = pl.BlockSpec(memory_space=pl.ANY)
    scratch = [pltpu.VMEM((2 * rows, depth), jnp.bfloat16)]
    if last:
        grads = resident(grads)
        outs, specs = jax.ShapeDtypeStruct(shape, jnp.float32), anywhere
        scratch += [
            pltpu.VMEM(shape, jnp.float32),
            pltpu.SemaphoreType.DMA((columns // 256, 2)),
        ]
    else:
        grads = pltpu.with_memory_space_constraint(grads, pltpu.HBM)
        outs, specs = [pltpu.VMEM(shape, jnp.float32)], [WHOLE]
        if ahead:
            outs.append(pltpu.VMEM((width, columns), grads.dtype))
            specs.append(WHOLE)
        scratch += [
            pltpu.VMEM((depth, columns), jnp.bfloat16),
            pltpu.SemaphoreType.DMA((len(shifts) * columns // 256 + 1,)),
        ]
    return pl.pallas_call(
        functools.partial(product_kernel, shifts, pieces, total is not None, last, ahead),
        in_specs=[SCALAR, SCALAR, *[WHOLE] * len(operands), WHOLE if last else anywhere],
        out_specs=specs,
        out_shape=outs,
        scratch_shapes=scratch,
        compiler_params=PARAMS,
    )(col, core, *map(resident, operands), grads)


def col_shift(value, shift):
    cols = lax.axis_size("cols")
    return lax.ppermute(value, "cols", [(c, (c + shift) % cols) for c in range(cols)])


def exchange(value):
    return lax.all_to_all(value, "rows", 0, 0, tiled=True)


def staged(hidden_acts, out_grads, row_signs, kept_index):
    row_devices = lax.axis_size("rows")
    cols = lax.axis_size("cols")
    block = lax.axis_index("rows")
    col = lax.axis_index("cols")[None]
    core = (block & 1)[None]
    pad_rows = PADDED // row_devices
    _, tokens = hidden_acts.shape[1:]
    share = kept_index.shape[0] // row_devices
    group = tokens // cols
    tiles = group // LANES
    grads = out_grads[0]

    table = jnp.asarray(sylvester(pad_rows // 2), dtype=jnp.bfloat16)
    segments = inner(
        col,
        table,
        row_signs[None],
        kept_index.reshape(-1, LANES),
        hidden_acts,
        row_devices,
        group,
    )
    segments = exchange(segments.reshape(row_devices, 1, -1)).reshape(-1, LANES)

    gradient = jnp.dot(hidden_acts[0], grads, preferred_element_type=jnp.float32)
    squares = jnp.sum(gradient * gradient)
    squares = jnp.broadcast_to(squares, (SUBLANES, LANES))
    steps = [("y", 1, "cols"), ("y", 2, "cols"), ("c", 1, "rows"), ("x", 16, "rows")]
    steps += [("x", 32, "rows"), ("z", 2, "rows"), ("z", 4, "rows"), ("z", 8, "rows")]
    for name, mask, axis in steps:
        other = lax.ppermute(
            squares, axis, [(i, i ^ mask) for i in range(lax.axis_size(axis))]
        )
        if (name, mask) != steps[-1][:2]:
            squares = squares + other

    cores = [list(range(core, row_devices, 2)) for core in range(2)]
    kept = mix(block[None], segments, row_devices, share, tiles, 0, group)
    kept = lax.all_to_all(kept, "rows", 0, 0, axis_index_groups=cores, tiled=True)

    half = row_devices // 2 * share
    top = kept[:, :share].reshape(half, group)
    low = kept[:, share:].reshape(half, group)
    low = lax.ppermute(low, "rows", [(i, i ^ 1) for i in range(row_devices)])
    up_top = col_shift(top, 1)
    down_low = col_shift(low, -1)
    up_low = col_shift(low, 1)
    down_top = col_shift(top, -1)
    part = half // 2
    far = [col_shift(up_top[:part], 1)]
    far.append(col_shift(down_top[part:], -1))
    far.append(col_shift(up_low[:part], 1))
    far.append(col_shift(down_low[part:], -1))
    (total,) = product(col, core, {0: (top, low)}, grads)
    parts = {1: (up_top, up_low), cols - 1: (down_top, down_low)}
    total, rows = product(col, core, parts, grads, total, ahead=2)
    total = product(col, core, {2: far}, rows, total, (squares, other))
    return total[None]


def solution(mesh):
    return jax.shard_map(
        staged,
        mesh=mesh,
        in_specs=(P(None, "rows", None), P(None, None, "cols"), P("rows"), P("rows")),
        out_specs=P(None, "rows", "cols"),
        check_vma=False,
    )
```

```python
import functools

import jax
import jax.numpy as jnp
import numpy as np
from jax import lax
from jax.experimental import pallas as pl
from jax.experimental.pallas import tpu as pltpu
from jax.sharding import PartitionSpec as P


D = 5120
PADDED = 32768

epsilon = 1e-06


def sylvester(length):
    i = np.arange(length)
    common = i[:, None] & i[None, :]
    parity = np.zeros_like(common)
    for bit in range(length.bit_length() - 1):
        parity ^= common >> bit & 1
    return 1 - 2 * parity


LANES = 128
SUBLANES = 8

WHOLE = pl.BlockSpec(memory_space=pltpu.VMEM)
SCALAR = pl.BlockSpec(memory_space=pltpu.SMEM)
PARAMS = pltpu.CompilerParams(vmem_limit_bytes=24 * 2**20)


def resident(value):
    return pltpu.with_memory_space_constraint(value, pltpu.VMEM)


def butterfly(rows):
    count = len(rows)
    bit = 1
    while bit < count:
        rows = [
            rows[i ^ bit] - rows[i] if i & bit else rows[i] + rows[i ^ bit]
            for i in range(count)
        ]
        bit *= 2
    return rows


def inner_kernel(blocks, col_ref, table_ref, signs_ref, kept_ref, acts_ref, out_ref):
    tiles = acts_ref.shape[2] // LANES
    own_rows = acts_ref.shape[1]
    stride = tiles * SUBLANES + 1
    signs = signs_ref[...].astype(jnp.float32).astype(jnp.bfloat16)
    size = table_ref.shape[0]
    halves = butterfly(
        [
            jnp.dot(
                table_ref[:, :min(own_rows - first, size)] * signs[:, first:first + size],
                acts_ref[0, first:first + size],
                preferred_element_type=jnp.float32,
            )
            for first in (0, size)
        ]
    )
    kept = kept_ref[...].astype(jnp.float32)
    share = kept.size // blocks
    for block in range(blocks):
        half, first = divmod(block * SUBLANES, size)
        for tile in range(tiles):
            out_ref[pl.ds(block * stride + tile * SUBLANES, SUBLANES), :] = halves[half][
                first:first + SUBLANES, tile * LANES:(tile + 1) * LANES
            ]
        row = block * share // LANES
        out_ref[pl.ds((block + 1) * stride - 1, 1), :] = kept[row:row + 1]


def inner(col, table, signs, kept, acts, blocks, width):
    own_rows = acts.shape[1]
    rows = blocks * (width // LANES * SUBLANES + 1)
    return pl.pallas_call(
        functools.partial(inner_kernel, blocks),
        grid_spec=pltpu.PrefetchScalarGridSpec(
            num_scalar_prefetch=1,
            grid=(1,),
            in_specs=[
                pl.BlockSpec(table.shape, lambda i, c: (0, 0)),
                pl.BlockSpec(signs.shape, lambda i, c: (0, 0)),
                pl.BlockSpec(kept.shape, lambda i, c: (0, 0)),
                pl.BlockSpec((1, own_rows, width), lambda i, c: (0, 0, c[0])),
            ],
            out_specs=WHOLE,
        ),
        out_shape=pltpu.VMEM((rows, LANES), jnp.float32),
        compiler_params=PARAMS,
    )(col, *[pltpu.with_memory_space_constraint(v, pltpu.HBM) for v in (table, signs, kept, acts)])


def mix_kernel(first, tiles, block_ref, segments_ref, kept_ref, position_ref, work_ref):
    blocks, share, width = kept_ref.shape
    low_count = blocks // 8
    stride = tiles * SUBLANES + 1

    sublane = lax.broadcasted_iota(jnp.int32, (SUBLANES, LANES), 0)
    lane = lax.rem(block_ref[0], LANES // share) * share + jnp.minimum(sublane, share - 1)
    for block in range(blocks):
        row = segments_ref[pl.ds((block + 1) * stride - 1, 1), :]
        row = jnp.broadcast_to(row, (SUBLANES, LANES)).astype(jnp.int32) & (SUBLANES - 1)
        position_ref[block] = jnp.take_along_axis(
            row, lane, axis=1, mode="promise_in_bounds"
        )

    for tile in range(width // LANES):
        at = slice(tile * LANES, (tile + 1) * LANES)
        for high in range(8):
            rows = butterfly(
                [
                    segments_ref[
                        pl.ds(
                            (high * low_count + low) * stride + (first + tile) * SUBLANES,
                            SUBLANES,
                        ),
                        :,
                    ]
                    for low in range(low_count)
                ]
            )
            for low in range(low_count):
                work_ref[high * low_count + low] = rows[low]
        for low in range(low_count):
            rows = butterfly([work_ref[high * low_count + low] for high in range(8)])
            for high in range(8):
                block = high * low_count + low
                picked = jnp.take_along_axis(
                    rows[high], position_ref[block], axis=0, mode="promise_in_bounds"
                )
                kept_ref[block, :, at] = picked[:share]


def mix(block, segments, blocks, share, tiles, start, width):
    return pl.pallas_call(
        functools.partial(mix_kernel, start // LANES, tiles),
        in_specs=[SCALAR, WHOLE],
        out_specs=WHOLE,
        out_shape=pltpu.VMEM((blocks, share, width), jnp.float32),
        compiler_params=PARAMS,
        scratch_shapes=[
            pltpu.VMEM((blocks, SUBLANES, LANES), jnp.int32),
            pltpu.VMEM((blocks, SUBLANES, LANES), jnp.float32),
        ],
    )(block, resident(segments))


def product_kernel(shifts, adds, scales, ahead, col_ref, *refs):
    count = len(shifts)
    parts, refs = refs[:2 * count], refs[2 * count:]
    total_ref, refs = (refs[0], refs[1:]) if adds else (None, refs)
    squares, refs = (refs[:2], refs[2:]) if scales else (None, refs)
    grads_ref, refs = refs[0], refs[1:]
    if scales:
        out_ref, terms_ref, done_ref, sems = refs
        rows_ref = grads_ref
    else:
        ahead_ref, refs = (refs[1], refs[:1] + refs[2:]) if ahead else (None, refs)
        out_ref, terms_ref, rows_ref, rows_sems = refs
    half, width = parts[0].shape
    rows = 2 * half
    columns = grads_ref.shape[1]
    widths = (640, 384, 256) if scales else (columns,)
    starts = [sum(widths[:i]) for i in range(len(widths))]
    tiles = [slice(start, start + span) for start, span in zip(starts, widths)]

    def fetch(shift, at, out, sem):
        groups = grads_ref.shape[0] // width
        source = lax.rem(col_ref[0] + groups - shift, groups)
        copy = pltpu.make_async_copy(
            grads_ref.at[pl.ds(pl.multiple_of(source * width, LANES), width), at], out, sem
        )
        copy.start()
        return copy

    fetches = [
        fetch(
            shift,
            at,
            rows_ref.at[i * width:(i + 1) * width, at],
            rows_sems.at[index * count + i],
        )
        for index, at in enumerate(tiles)
        for i, shift in enumerate(shifts)
        if not scales
    ]
    if ahead:
        later = fetch(ahead, slice(None), ahead_ref, rows_sems.at[len(fetches)])

    for i, part in enumerate(parts):
        value = part[...]
        coarse = value.astype(jnp.bfloat16)
        at = slice(i // 2 * width, (i // 2 + 1) * width)
        first = i % 2 * half
        terms_ref[first:first + half, at] = coarse
        terms_ref[rows + first:rows + first + half, at] = (
            value - coarse.astype(jnp.float32)
        ).astype(jnp.bfloat16)

    if scales:
        squares = squares[0][:1] + squares[1][:1]
        scale = jnp.tile(lax.rsqrt(squares / D + epsilon), (1, columns // LANES))
    copies = []
    for index, at in enumerate(tiles):
        for copy in fetches[index * count:(index + 1) * count]:
            copy.wait()
        both = jnp.dot(terms_ref[...], rows_ref[:, at], preferred_element_type=jnp.float32)
        value = both[:rows] + both[rows:]
        if adds:
            value = value + total_ref[:, at]
        if not scales:
            out_ref[:, at] = value
            continue
        done_ref[:, at] = value * scale[:, at]
        copies.append(pltpu.make_async_copy(done_ref.at[:, at], out_ref.at[:, at], sems.at[index]))
        copies[-1].start()
    for copy in copies:
        copy.wait()
    if ahead:
        later.wait()


def product(col, parts, grads, total=None, squares=None, ahead=None):
    shifts = tuple(parts)
    last = squares is not None
    halves = [half for shift in shifts for half in parts[shift]]
    half, width = halves[0].shape
    columns = grads.shape[1]
    depth = len(shifts) * width
    operands = [*halves, *([] if total is None else [total]), *(squares or ())]
    shape = (2 * half, columns)
    anywhere = pl.BlockSpec(memory_space=pl.ANY)
    scratch = [pltpu.VMEM((4 * half, depth), jnp.bfloat16)]
    if last:
        grads = resident(grads)
        outs, specs = jax.ShapeDtypeStruct(shape, jnp.float32), anywhere
        scratch += [
            pltpu.VMEM(shape, jnp.float32),
            pltpu.SemaphoreType.DMA((columns // 256,)),
        ]
    else:
        grads = pltpu.with_memory_space_constraint(grads, pltpu.HBM)
        outs, specs = [pltpu.VMEM(shape, jnp.float32)], [WHOLE]
        if ahead:
            outs.append(pltpu.VMEM((width, columns), grads.dtype))
            specs.append(WHOLE)
        scratch += [
            pltpu.VMEM((depth, columns), jnp.bfloat16),
            pltpu.SemaphoreType.DMA((len(shifts) * columns // 256 + 1,)),
        ]
    return pl.pallas_call(
        functools.partial(product_kernel, shifts, total is not None, last, ahead),
        in_specs=[SCALAR, *[WHOLE] * len(operands), WHOLE if last else anywhere],
        out_specs=specs,
        out_shape=outs,
        scratch_shapes=scratch,
        compiler_params=PARAMS,
    )(col, *map(resident, operands), grads)


def col_shift(value, shift):
    cols = lax.axis_size("cols")
    return lax.ppermute(value, "cols", [(c, (c + shift) % cols) for c in range(cols)])


def exchange(value):
    return lax.all_to_all(value, "rows", 0, 0, tiled=True)


def staged(hidden_acts, out_grads, row_signs, kept_index):
    row_devices = lax.axis_size("rows")
    cols = lax.axis_size("cols")
    block = lax.axis_index("rows")
    col = lax.axis_index("cols")[None]
    pad_rows = PADDED // row_devices
    _, tokens = hidden_acts.shape[1:]
    share = kept_index.shape[0] // row_devices
    group = tokens // cols
    tiles = group // LANES
    grads = out_grads[0]

    table = jnp.asarray(sylvester(pad_rows // 2), dtype=jnp.bfloat16)
    segments = inner(
        col,
        table,
        row_signs[None],
        kept_index.reshape(-1, LANES),
        hidden_acts,
        row_devices,
        group,
    )
    segments = exchange(segments.reshape(row_devices, 1, -1)).reshape(-1, LANES)

    gradient = jnp.dot(hidden_acts[0], grads, preferred_element_type=jnp.float32)
    squares = jnp.sum(gradient * gradient)
    squares = jnp.broadcast_to(squares, (SUBLANES, LANES))
    steps = [("y", 1, "cols"), ("y", 2, "cols"), ("c", 1, "rows"), ("x", 16, "rows")]
    steps += [("x", 32, "rows"), ("z", 2, "rows"), ("z", 4, "rows"), ("z", 8, "rows")]
    for name, mask, axis in steps:
        other = lax.ppermute(
            squares, axis, [(i, i ^ mask) for i in range(lax.axis_size(axis))]
        )
        if (name, mask) != steps[-1][:2]:
            squares = squares + other

    kept = mix(block[None], segments, row_devices, share, tiles, 0, group)
    kept = exchange(kept)

    half = row_devices // 2
    top = kept[:half].reshape(half * share, group)
    low = kept[half:].reshape(half * share, group)
    up_top = col_shift(top, 1)
    down_low = col_shift(low, -1)
    up_low = col_shift(low, 1)
    down_top = col_shift(top, -1)
    far_top = col_shift(up_top, 1)
    far_low = col_shift(down_low, -1)
    (total,) = product(col, {0: (top, low)}, grads)
    parts = {1: (up_top, up_low), cols - 1: (down_top, down_low)}
    total, rows = product(col, parts, grads, total, ahead=2)
    total = product(col, {2: (far_top, far_low)}, rows, total, (squares, other))
    return total[None]


def solution(mesh):
    return jax.shard_map(
        staged,
        mesh=mesh,
        in_specs=(P(None, "rows", None), P(None, None, "cols"), P("rows"), P("rows")),
        out_specs=P(None, "rows", "cols"),
        check_vma=False,
    )
```

```python
import functools

import jax
import jax.numpy as jnp
import numpy as np
from jax import lax
from jax.experimental import pallas as pl
from jax.experimental.pallas import tpu as pltpu
from jax.sharding import PartitionSpec as P


D = 5120
PADDED = 32768

epsilon = 1e-06


def sylvester(length):
    i = np.arange(length)
    common = i[:, None] & i[None, :]
    parity = np.zeros_like(common)
    for bit in range(length.bit_length() - 1):
        parity ^= common >> bit & 1
    return 1 - 2 * parity


LANES = 128
SUBLANES = 8

WHOLE = pl.BlockSpec(memory_space=pltpu.VMEM)
SCALAR = pl.BlockSpec(memory_space=pltpu.SMEM)
PARAMS = pltpu.CompilerParams(vmem_limit_bytes=24 * 2**20)


def resident(value):
    return pltpu.with_memory_space_constraint(value, pltpu.VMEM)


def butterfly(rows):
    count = len(rows)
    bit = 1
    while bit < count:
        rows = [
            rows[i ^ bit] - rows[i] if i & bit else rows[i] + rows[i ^ bit]
            for i in range(count)
        ]
        bit *= 2
    return rows


def inner_kernel(
    blocks, col_ref, table_ref, signs_ref, kept_ref, acts_ref, out_ref, done_ref, sems
):
    tiles = acts_ref.shape[2] // LANES
    own_rows = acts_ref.shape[1]
    stride = tiles * SUBLANES + 1
    signs = signs_ref[...].astype(jnp.float32).astype(jnp.bfloat16)
    size = table_ref.shape[0]
    halves = butterfly(
        [
            jnp.dot(
                table_ref[:, :min(own_rows - first, size)] * signs[:, first:first + size],
                acts_ref[0, first:first + size],
                preferred_element_type=jnp.float32,
            )
            for first in (0, size)
        ]
    )
    kept = kept_ref[...].astype(jnp.float32)
    share = kept.size // blocks
    copies = []
    run = blocks // sems.shape[0]
    for block in range(blocks):
        half, first = divmod(block * SUBLANES, size)
        for tile in range(tiles):
            done_ref[pl.ds(block * stride + tile * SUBLANES, SUBLANES), :] = halves[half][
                first:first + SUBLANES, tile * LANES:(tile + 1) * LANES
            ]
        row = block * share // LANES
        done_ref[pl.ds((block + 1) * stride - 1, 1), :] = kept[row:row + 1]
        if (block + 1) % run == 0:
            part = pl.ds((block + 1 - run) * stride, run * stride)
            copies.append(
                pltpu.make_async_copy(done_ref.at[part], out_ref.at[part], sems.at[block // run])
            )
            copies[-1].start()
    for copy in copies:
        copy.wait()


def inner(col, table, signs, kept, acts, blocks, width):
    own_rows = acts.shape[1]
    rows = blocks * (width // LANES * SUBLANES + 1)
    return pl.pallas_call(
        functools.partial(inner_kernel, blocks),
        grid_spec=pltpu.PrefetchScalarGridSpec(
            num_scalar_prefetch=1,
            grid=(1,),
            in_specs=[
                pl.BlockSpec(table.shape, lambda i, c: (0, 0)),
                pl.BlockSpec(signs.shape, lambda i, c: (0, 0)),
                pl.BlockSpec(kept.shape, lambda i, c: (0, 0)),
                pl.BlockSpec((1, own_rows, width), lambda i, c: (0, 0, c[0])),
            ],
            out_specs=pl.BlockSpec(memory_space=pl.ANY),
            scratch_shapes=[
                pltpu.VMEM((rows, LANES), jnp.float32),
                pltpu.SemaphoreType.DMA((4,)),
            ],
        ),
        out_shape=jax.ShapeDtypeStruct((rows, LANES), jnp.float32),
        compiler_params=PARAMS,
    )(col, *[pltpu.with_memory_space_constraint(v, pltpu.HBM) for v in (table, signs, kept, acts)])


def mix_kernel(first, tiles, block_ref, segments_ref, kept_ref, position_ref, work_ref):
    blocks, share, width = kept_ref.shape
    low_count = blocks // 8
    stride = tiles * SUBLANES + 1

    sublane = lax.broadcasted_iota(jnp.int32, (SUBLANES, LANES), 0)
    lane = lax.rem(block_ref[0], LANES // share) * share + jnp.minimum(sublane, share - 1)
    for block in range(blocks):
        row = segments_ref[pl.ds((block + 1) * stride - 1, 1), :]
        row = jnp.broadcast_to(row, (SUBLANES, LANES)).astype(jnp.int32) & (SUBLANES - 1)
        position_ref[block] = jnp.take_along_axis(
            row, lane, axis=1, mode="promise_in_bounds"
        )

    for tile in range(width // LANES):
        at = slice(tile * LANES, (tile + 1) * LANES)
        for high in range(8):
            rows = butterfly(
                [
                    segments_ref[
                        pl.ds(
                            (high * low_count + low) * stride + (first + tile) * SUBLANES,
                            SUBLANES,
                        ),
                        :,
                    ]
                    for low in range(low_count)
                ]
            )
            for low in range(low_count):
                work_ref[high * low_count + low] = rows[low]
        for low in range(low_count):
            rows = butterfly([work_ref[high * low_count + low] for high in range(8)])
            for high in range(8):
                block = high * low_count + low
                picked = jnp.take_along_axis(
                    rows[high], position_ref[block], axis=0, mode="promise_in_bounds"
                )
                kept_ref[block, :, at] = picked[:share]


def mix(block, segments, blocks, share, tiles, start, width):
    return pl.pallas_call(
        functools.partial(mix_kernel, start // LANES, tiles),
        in_specs=[SCALAR, WHOLE],
        out_specs=WHOLE,
        out_shape=pltpu.VMEM((blocks, share, width), jnp.float32),
        compiler_params=PARAMS,
        scratch_shapes=[
            pltpu.VMEM((blocks, SUBLANES, LANES), jnp.int32),
            pltpu.VMEM((blocks, SUBLANES, LANES), jnp.float32),
        ],
    )(block, resident(segments))


def product_kernel(shifts, adds, scales, ahead, col_ref, *refs):
    count = len(shifts)
    parts, refs = refs[:2 * count], refs[2 * count:]
    total_ref, refs = (refs[0], refs[1:]) if adds else (None, refs)
    squares, refs = (refs[:2], refs[2:]) if scales else (None, refs)
    grads_ref, refs = refs[0], refs[1:]
    if scales:
        out_ref, terms_ref, done_ref, sems = refs
        rows_ref = grads_ref
    else:
        ahead_ref, refs = (refs[1], refs[:1] + refs[2:]) if ahead else (None, refs)
        out_ref, terms_ref, rows_ref, rows_sems = refs
    half, width = parts[0].shape
    rows = 2 * half
    columns = grads_ref.shape[1]
    tile = 256
    tiles = [slice(first, first + tile) for first in range(0, columns, tile)]

    def fetch(shift, at, out, sem):
        groups = grads_ref.shape[0] // width
        source = lax.rem(col_ref[0] + groups - shift, groups)
        copy = pltpu.make_async_copy(
            grads_ref.at[pl.ds(pl.multiple_of(source * width, LANES), width), at], out, sem
        )
        copy.start()
        return copy

    fetches = [
        fetch(
            shift,
            at,
            rows_ref.at[i * width:(i + 1) * width, at],
            rows_sems.at[index * count + i],
        )
        for index, at in enumerate(tiles)
        for i, shift in enumerate(shifts)
        if not scales
    ]
    if ahead:
        later = fetch(ahead, slice(None), ahead_ref, rows_sems.at[len(fetches)])

    for i, part in enumerate(parts):
        value = part[...]
        coarse = value.astype(jnp.bfloat16)
        at = slice(i // 2 * width, (i // 2 + 1) * width)
        first = i % 2 * half
        terms_ref[first:first + half, at] = coarse
        terms_ref[rows + first:rows + first + half, at] = (
            value - coarse.astype(jnp.float32)
        ).astype(jnp.bfloat16)

    if scales:
        squares = squares[0][:1] + squares[1][:1]
        scale = jnp.tile(lax.rsqrt(squares / D + epsilon), (1, tile // LANES))
    copies = []
    for index, at in enumerate(tiles):
        for copy in fetches[index * count:(index + 1) * count]:
            copy.wait()
        both = jnp.dot(terms_ref[...], rows_ref[:, at], preferred_element_type=jnp.float32)
        value = both[:rows] + both[rows:]
        if adds:
            value = value + total_ref[:, at]
        if not scales:
            out_ref[:, at] = value
            continue
        done_ref[:, at] = value * scale
        copies.append(pltpu.make_async_copy(done_ref.at[:, at], out_ref.at[:, at], sems.at[index]))
        copies[-1].start()
    for copy in copies:
        copy.wait()
    if ahead:
        later.wait()


def product(col, parts, grads, total=None, squares=None, ahead=None):
    shifts = tuple(parts)
    last = squares is not None
    halves = [half for shift in shifts for half in parts[shift]]
    half, width = halves[0].shape
    columns = grads.shape[1]
    depth = len(shifts) * width
    operands = [*halves, *([] if total is None else [total]), *(squares or ())]
    shape = (2 * half, columns)
    anywhere = pl.BlockSpec(memory_space=pl.ANY)
    scratch = [pltpu.VMEM((4 * half, depth), jnp.bfloat16)]
    if last:
        grads = resident(grads)
        outs, specs = jax.ShapeDtypeStruct(shape, jnp.float32), anywhere
        scratch += [
            pltpu.VMEM(shape, jnp.float32),
            pltpu.SemaphoreType.DMA((columns // 256,)),
        ]
    else:
        grads = pltpu.with_memory_space_constraint(grads, pltpu.HBM)
        outs, specs = [pltpu.VMEM(shape, jnp.float32)], [WHOLE]
        if ahead:
            outs.append(pltpu.VMEM((width, columns), grads.dtype))
            specs.append(WHOLE)
        scratch += [
            pltpu.VMEM((depth, columns), jnp.bfloat16),
            pltpu.SemaphoreType.DMA((len(shifts) * columns // 256 + 1,)),
        ]
    return pl.pallas_call(
        functools.partial(product_kernel, shifts, total is not None, last, ahead),
        in_specs=[SCALAR, *[WHOLE] * len(operands), WHOLE if last else anywhere],
        out_specs=specs,
        out_shape=outs,
        scratch_shapes=scratch,
        compiler_params=PARAMS,
    )(col, *map(resident, operands), grads)


def col_shift(value, shift):
    cols = lax.axis_size("cols")
    return lax.ppermute(value, "cols", [(c, (c + shift) % cols) for c in range(cols)])


def exchange(value):
    return lax.all_to_all(value, "rows", 0, 0, tiled=True)


def staged(hidden_acts, out_grads, row_signs, kept_index):
    row_devices = lax.axis_size("rows")
    cols = lax.axis_size("cols")
    block = lax.axis_index("rows")
    col = lax.axis_index("cols")[None]
    pad_rows = PADDED // row_devices
    _, tokens = hidden_acts.shape[1:]
    share = kept_index.shape[0] // row_devices
    group = tokens // cols
    tiles = group // LANES
    grads = out_grads[0]

    table = jnp.asarray(sylvester(pad_rows // 2), dtype=jnp.bfloat16)
    segments = inner(
        col,
        table,
        row_signs[None],
        kept_index.reshape(-1, LANES),
        hidden_acts,
        row_devices,
        group,
    )
    segments = exchange(segments.reshape(row_devices, 1, -1)).reshape(-1, LANES)

    gradient = jnp.dot(hidden_acts[0], grads, preferred_element_type=jnp.float32)
    squares = jnp.sum(gradient * gradient)
    squares = jnp.broadcast_to(squares, (SUBLANES, LANES))
    steps = [("y", 1, "cols"), ("y", 2, "cols"), ("c", 1, "rows"), ("x", 16, "rows")]
    steps += [("x", 32, "rows"), ("z", 2, "rows"), ("z", 4, "rows"), ("z", 8, "rows")]
    for name, mask, axis in steps:
        other = lax.ppermute(
            squares, axis, [(i, i ^ mask) for i in range(lax.axis_size(axis))]
        )
        if (name, mask) != steps[-1][:2]:
            squares = squares + other

    kept = mix(block[None], segments, row_devices, share, tiles, 0, group)
    kept = exchange(kept)

    half = row_devices // 2
    top = kept[:half].reshape(half * share, group)
    low = kept[half:].reshape(half * share, group)
    up_top = col_shift(top, 1)
    down_low = col_shift(low, -1)
    up_low = col_shift(low, 1)
    down_top = col_shift(top, -1)
    far_top = col_shift(up_top, 1)
    far_low = col_shift(down_low, -1)
    (total,) = product(col, {0: (top, low)}, grads)
    parts = {1: (up_top, up_low), cols - 1: (down_top, down_low)}
    total, rows = product(col, parts, grads, total, ahead=2)
    total = product(col, {2: (far_top, far_low)}, rows, total, (squares, other))
    return total[None]


def solution(mesh):
    return jax.shard_map(
        staged,
        mesh=mesh,
        in_specs=(P(None, "rows", None), P(None, None, "cols"), P("rows"), P("rows")),
        out_specs=P(None, "rows", "cols"),
        check_vma=False,
    )
```
